256 devices in a mesh: samp: 32 (over z, x), var: 8 (over y, core).
Axes of the slice: x: 4, y: 4, z: 8, core: 2. Of those that a mesh axis runs over, the one named last changes fastest.
Arguments:
- genotypes: bfloat16 [65536, 24576], P('samp', 'var'), as said below
- residuals: bfloat16 [65536, 4], P('samp')
- weights: bfloat16 [65536, 4], P('samp'), may hold values from 0.049804688 to 0.25
- block_regions: int32 [192], P('var'), may hold values from 0 to 1
- leads: int32 [16, 64], replicated, may hold values from 0 to 24575, as said below
Outputs:
- scores: float32 [4, 24576], P(None, 'var')
- variances: float32 [4, 24576], P(None, 'var')
The draws below stay inside these ranges and needn't reach their ends.
Inputs may be any that keep to these rules, and one draw needn't show every extreme that they name: `block_regions`: each index of var owns 2 regions; a block names one of the regions owned by the var index that holds it. The 128 leads of the regions of one var index are distinct; at most 32 of them lie among the variants of any one var index, and exactly 32 lie on some var index. `genotypes`: dosages and weights are such that every gram is positive definite.
All inputs are finite; a program needn't handle non-finite values.
Results may differ from the reference program's by a relative error of at most 0.002.
Values may be sent and summed in bfloat16 or wider, within the bound.
A program may use at most 128 MiB of HBM per device.

```python
import math
import jax
import jax.numpy as jnp
from jax import lax

MV_DEV = 3072
VB = 128
REG_DEV = 2
L = 64
K = 4
HOST = 32
NS = 65536
M = 24576
REGIONS = 16
NBLK = 192


def shared_factor(key):
    return jax.random.normal(jax.random.fold_in(key, 1), (NS,), jnp.float32)


def draw_genotypes(key, part):
    noise_key = jax.random.fold_in(key, 3)
    load_key = jax.random.fold_in(key, 5)
    loadings = jax.random.uniform(load_key, (M,), jnp.float32, 0.1, 0.4)
    noise = jax.random.normal(noise_key, (NS, M), jnp.float32)
    return (noise + shared_factor(key)[:, None] * loadings[None, :]).astype(jnp.bfloat16)


def draw_residuals(key, part):
    noise_key = jax.random.fold_in(key, 7)
    load_key = jax.random.fold_in(key, 9)
    loadings = jnp.exp(jax.random.uniform(load_key, (K,), jnp.float32, jnp.log(0.02), jnp.log(0.08)))
    noise = jax.random.normal(noise_key, (NS, K), jnp.float32)
    return (noise + shared_factor(key)[:, None] * loadings[None, :]).astype(jnp.bfloat16)


def draw_leads(key, part):
    slots_all = REG_DEV * L
    owners = REGIONS // REG_DEV

    def for_owner(owner):
        owner_key = jax.random.fold_in(key, owner + 11)
        key_first, key_mixed, key_local, key_order = jax.random.split(owner_key, 4)
        first = jax.random.randint(key_first, (), 0, owners)
        others = (first + 1 + jnp.arange((owners - 1) * HOST, dtype=jnp.int32) // HOST) % owners
        mixed = jax.random.permutation(key_mixed, others)[:slots_all - HOST]
        source = jnp.concatenate([jnp.full((HOST,), first, jnp.int32), mixed.astype(jnp.int32)])
        onehot = (source[:, None] == jnp.arange(owners, dtype=jnp.int32)[None, :]).astype(jnp.int32)
        ranked = jnp.sum((jnp.cumsum(onehot, axis=0) - 1) * onehot, axis=1)
        drawn = jax.vmap(lambda single: jax.random.permutation(single, MV_DEV))(jax.random.split(key_local, owners))
        offset = drawn[source, ranked].astype(jnp.int32)
        shuffle = jax.random.permutation(key_order, slots_all)
        return (source * MV_DEV + offset)[shuffle].reshape(REG_DEV, L)
    return jax.vmap(for_owner)(jnp.arange(owners, dtype=jnp.int32)).reshape(REGIONS, L).astype(jnp.int32)


def with_ends(values, rng, low, top_value):
    longest = values.shape.index(max(values.shape))
    spots = []
    for shift in (0, 1):
        where = [jax.random.randint(jax.random.fold_in(rng, axis), (), 0, length) for axis, length in enumerate(values.shape)]
        where[longest] = (where[longest] + shift) % values.shape[longest]
        spots.append(tuple(where))
    return values.at[spots[0]].set(low).at[spots[1]].set(top_value)


def steps_of(stream_key, shape, shards, smallest, largest):
    def one(dim, parts):
        steps = jax.random.uniform(jax.random.fold_in(jax.random.fold_in(stream_key, 6), dim), (parts,), jnp.float32, smallest / len(shards), largest / len(shards))
        return jnp.repeat(jnp.exp(steps), shape[dim] // parts).reshape((-1,) + (1,) * (len(shape) - dim - 1))

    gain = one(*shards[0])
    for cut in shards[1:]:
        gain = gain * one(*cut)
    return gain


def setup_inputs(seed: int = 0) -> dict:
    key_list = jax.random.split(jax.random.key(seed), 6)
    return {
        "genotypes": draw_genotypes(jax.random.fold_in(key_list[5], 71), 0),
        "residuals": draw_residuals(jax.random.fold_in(key_list[5], 71), 0),
        "weights": jnp.clip(0.049804688 + 0.20019531 * jax.random.uniform(key_list[2], (NS, K), jnp.float32) ** steps_of(key_list[2], (NS, K), ((0, 32),), -0.2, 0.2), 0.049804688, 0.25).astype(jnp.bfloat16),
        "block_regions": with_ends(jax.random.randint(key_list[3], (NBLK,), 0, REG_DEV), jax.random.fold_in(key_list[3], 1), 0, REG_DEV - 1).astype(jnp.int32),
        "leads": draw_leads(jax.random.fold_in(key_list[5], 71), 0),
    }


def region_stats(genotypes, residuals, weights, lead_list):
    columns = jnp.take(genotypes, lead_list, axis=1)
    weighted = (columns.astype(jnp.float32)[:, None, :] * weights.astype(jnp.float32)[:, :, None]).astype(jnp.bfloat16)
    gram = jnp.einsum('skl,sm->klm', weighted.astype(jnp.float32), columns.astype(jnp.float32), precision=lax.Precision.HIGHEST)
    lead_score = jnp.einsum('sl,sk->kl', columns.astype(jnp.float32), residuals.astype(jnp.float32), precision=lax.Precision.HIGHEST)
    return (weighted, gram, lead_score)

def reference(genotypes, residuals, weights, block_regions, leads):
    blocks_dev = MV_DEV // VB

    def per_region(region):
        unused, gram, lead_score = region_stats(genotypes, residuals, weights, leads[region])
        return (gram, lead_score)
    grams, lead_scores = lax.map(per_region, jnp.arange(REGIONS, dtype=jnp.int32))
    chol = jnp.linalg.cholesky(grams)
    lead_solved = jax.scipy.linalg.solve_triangular(chol, lead_scores[..., None], lower=True)[..., 0]

    def per_block(block):
        region = block // blocks_dev * REG_DEV + block_regions[block]
        weighted, unused_gram, unused_score = region_stats(genotypes, residuals, weights, leads[region])
        weighted = weighted.reshape(NS, K * L)
        block_cols = lax.dynamic_slice_in_dim(genotypes, block * VB, VB, 1)
        cross = jnp.dot(block_cols.T.astype(jnp.float32), weighted.astype(jnp.float32), preferred_element_type=jnp.float32).reshape(VB, K, L)
        score = jnp.dot(block_cols.T.astype(jnp.float32), residuals.astype(jnp.float32), preferred_element_type=jnp.float32)
        squared = jnp.square(block_cols.astype(jnp.float32)).astype(jnp.bfloat16)
        diag = jnp.dot(squared.T.astype(jnp.float32), weights.astype(jnp.float32), preferred_element_type=jnp.float32)
        solved = jax.scipy.linalg.solve_triangular(chol[region], jnp.transpose(cross, (1, 2, 0)), lower=True)
        tstat = (score.T - jnp.einsum('klj,kl->kj', solved, lead_solved[region], precision=lax.Precision.HIGHEST)) / math.sqrt(NS)
        varv = (diag.T - lax.optimization_barrier(jnp.sum(solved * solved, axis=1))) / NS
        return (tstat, varv)
    tstats, varvs = lax.map(per_block, jnp.arange(NBLK, dtype=jnp.int32))
    scores = jnp.transpose(tstats, (1, 0, 2)).reshape(K, M)
    variances = jnp.transpose(varvs, (1, 0, 2)).reshape(K, M)
    return (scores, variances)
```

```python
import functools
import math

import jax
import jax.numpy as jnp
from jax import lax
from jax.experimental import pallas as pl
from jax.experimental.pallas import tpu as pltpu
from jax.sharding import PartitionSpec as P

VB = 128
HOST = 32
NT = (((1,), (1,)), ((), ()))
NN = (((1,), (0,)), ((), ()))
EXTRA = 16


def gather_kernel(listed_ref, geno_ref, out_ref, onehot):
    nvar, slots = listed_ref.shape
    local_vars = geno_ref.shape[1]

    @pl.when(pl.program_id(0) == 0)
    def _():
        base = lax.axis_index("var") * local_vars
        offset = listed_ref[...] - base
        hosted = (offset >= 0) & (offset < local_vars)
        before = lax.broadcasted_iota(jnp.int32, (slots, slots), 0) < lax.broadcasted_iota(
            jnp.int32, (slots, slots), 1
        )
        rank = lax.dot_general(
            hosted.astype(jnp.float32),
            before.astype(jnp.float32),
            NN,
            preferred_element_type=jnp.float32,
        ).astype(jnp.int32)
        rank = jnp.where(hosted, rank, HOST)
        place = lax.broadcasted_iota(jnp.int32, (HOST, slots), 0)
        lanes = lax.broadcasted_iota(jnp.int32, (HOST, local_vars), 1)
        for owner in range(nvar):
            match = rank[owner : owner + 1, :] == place
            picked = jnp.sum(
                jnp.where(match, offset[owner : owner + 1, :], 0), axis=1, keepdims=True
            )
            onehot[owner * HOST : (owner + 1) * HOST, :] = (
                (lanes == picked).astype(jnp.float32).astype(jnp.bfloat16)
            )

    out_ref[...] = lax.dot_general(
        onehot[...], geno_ref[...], NT, preferred_element_type=jnp.float32
    ).astype(jnp.bfloat16)


def gather(listed, genotypes, tile=256):
    samples, local_vars = genotypes.shape
    nvar, slots = listed.shape
    rows = nvar * HOST
    return pl.pallas_call(
        gather_kernel,
        grid=(samples // tile,),
        in_specs=[
            pl.BlockSpec((nvar, slots), lambda i: (0, 0)),
            pl.BlockSpec((tile, local_vars), lambda i: (i, 0)),
        ],
        out_specs=pl.BlockSpec((rows, tile), lambda i: (0, i)),
        out_shape=jax.ShapeDtypeStruct((rows, samples), jnp.bfloat16),
        scratch_shapes=[pltpu.VMEM((rows, local_vars), jnp.bfloat16)],
        name="lead_gather",
    )(listed, genotypes)


def cross_kernel(region_ref, slot_ref, incoming_ref, side_ref, geno_ref, out_ref, lead, weighted, gram):
    nregion, rows, samples = weighted.shape
    nlead = lead.shape[0] // nregion
    traits = (rows - EXTRA) // nlead
    chunk = geno_ref.shape[1]
    step = pl.program_id(0)

    @pl.when(step == 0)
    def _():
        slots = incoming_ref.shape[0]
        pick = (
            lax.broadcasted_iota(jnp.int32, (nregion * nlead, slots), 1) == slot_ref[...]
        ).astype(jnp.float32).astype(jnp.bfloat16)
        lead[...] = lax.dot_general(
            pick, incoming_ref[...], NN, preferred_element_type=jnp.float32
        ).astype(jnp.bfloat16)
        for region in range(nregion):
            cols = lead[region * nlead : (region + 1) * nlead, :].astype(jnp.float32)
            for trait in range(traits):
                scale = side_ref[EXTRA + trait : EXTRA + trait + 1, :].astype(jnp.float32)
                weighted[region, trait * nlead : (trait + 1) * nlead, :] = (cols * scale).astype(
                    jnp.bfloat16
                )
            weighted[region, traits * nlead :, :] = side_ref[:EXTRA, :]
            gram[region] = lax.dot_general(
                weighted[region],
                lead[region * nlead : (region + 1) * nlead, :],
                NT,
                preferred_element_type=jnp.float32,
            )

    per_chunk = chunk // VB
    for block in range(per_chunk):
        region = region_ref[step * per_chunk + block]
        cols = geno_ref[:, block * VB : (block + 1) * VB]
        acc = lax.dot_general(weighted[region], cols, NN, preferred_element_type=jnp.float32)
        square = cols.astype(jnp.float32)
        square = (square * square).astype(jnp.bfloat16)
        diag = lax.dot_general(
            side_ref[EXTRA:, :], square, NN, preferred_element_type=jnp.float32
        )
        here = slice(block * VB, (block + 1) * VB)
        for trait in range(traits):
            out_ref[0, trait, :nlead, here] = acc[trait * nlead : (trait + 1) * nlead, :]
            out_ref[0, trait, nlead : nlead + 1, here] = acc[
                traits * nlead + trait : traits * nlead + trait + 1, :
            ]
            out_ref[0, trait, nlead + 1 : nlead + 2, here] = diag[trait : trait + 1, :]
            out_ref[0, trait, nlead + 2 :, here] = jnp.zeros((6, VB), jnp.float32)
    for trait in range(traits):
        out_ref[0, trait, nlead:, chunk:] = jnp.zeros((8, 2 * nlead), jnp.float32)
        for region in range(nregion):
            there = slice(chunk + region * nlead, chunk + (region + 1) * nlead)
            out_ref[0, trait, :nlead, there] = gram[region, trait * nlead : (trait + 1) * nlead, :]
            out_ref[0, trait, nlead : nlead + 1, there] = gram[
                region, traits * nlead + trait : traits * nlead + trait + 1, :
            ]


def cross_products(regions, slot, incoming, side, genotypes, traits, nregion, nchunk):
    samples, local_vars = genotypes.shape
    nlead = slot.shape[0] // nregion
    chunk = local_vars // nchunk
    rows = traits * nlead + EXTRA
    whole = lambda i, r: (0, 0)
    shape = (nchunk, traits, nlead + 8, chunk + nregion * nlead)
    return pl.pallas_call(
        cross_kernel,
        grid_spec=pltpu.PrefetchScalarGridSpec(
            num_scalar_prefetch=1,
            grid=(nchunk,),
            in_specs=[
                pl.BlockSpec(slot.shape, whole),
                pl.BlockSpec(incoming.shape, whole),
                pl.BlockSpec(side.shape, whole),
                pl.BlockSpec((samples, chunk), lambda i, r: (0, i)),
            ],
            out_specs=pl.BlockSpec((1,) + shape[1:], lambda i, r: (i, 0, 0, 0)),
            scratch_shapes=[
                pltpu.VMEM((nregion * nlead, samples), jnp.bfloat16),
                pltpu.VMEM((nregion, rows, samples), jnp.bfloat16),
                pltpu.VMEM((nregion, rows, nlead), jnp.float32),
            ],
        ),
        out_shape=jax.ShapeDtypeStruct(shape, jnp.float32),
        compiler_params=pltpu.CompilerParams(vmem_limit_bytes=48 * 1024 * 1024),
        name="cross_products",
    )(regions, slot, incoming, side, genotypes)


def finish_kernel(traits, total, region_ref, sum_ref, out_ref, inverse, pivots, target):
    nregion, nlead, _ = inverse.shape
    chunk = out_ref.shape[1]
    per_chunk = chunk // VB
    first = (lax.axis_index("samp") // traits) * per_chunk
    eye = (
        lax.broadcasted_iota(jnp.int32, (nlead, nlead), 0)
        == lax.broadcasted_iota(jnp.int32, (nlead, nlead), 1)
    )
    unit = eye.astype(jnp.float32)
    below = lax.broadcasted_iota(jnp.int32, (nlead, 1), 0)
    state = [
        jnp.concatenate(
            [sum_ref[:nlead, chunk + r * nlead : chunk + (r + 1) * nlead], unit], axis=1
        )
        for r in range(nregion)
    ]
    for j in range(nlead - 1):
        for r in range(nregion):
            row = state[r][j : j + 1, :]
            ratio = state[r][:, j : j + 1] / row[:, j : j + 1]
            state[r] = state[r] - jnp.where(below > j, ratio, 0.0) * row
    for r in range(nregion):
        lower = state[r][:, nlead:]
        upper = state[r][:, :nlead]
        inverse[r] = lower
        pivot = 1.0 / jnp.sum(jnp.where(eye, upper, 0.0), axis=1, keepdims=True)
        score = sum_ref[nlead : nlead + 1, chunk + r * nlead : chunk + (r + 1) * nlead]
        pivots[r] = jnp.broadcast_to(pivot, (nlead, VB))
        target[r] = jnp.broadcast_to(
            jnp.sum(lower * score, axis=1, keepdims=True) * pivot, (nlead, VB)
        )
    out_ref[...] = jnp.zeros_like(out_ref)
    for block in range(per_chunk):
        here = slice(block * VB, (block + 1) * VB)
        region = region_ref[first + block]
        solved = lax.dot_general(
            inverse[region],
            sum_ref[:nlead, here],
            NN,
            preferred_element_type=jnp.float32,
            precision=lax.Precision.HIGHEST,
        )
        fit = jnp.sum(solved * target[region], axis=0, keepdims=True)
        used = jnp.sum(solved * solved * pivots[region], axis=0, keepdims=True)
        out_ref[0:1, here] = (sum_ref[nlead : nlead + 1, here] - fit) / math.sqrt(total)
        out_ref[1:2, here] = (sum_ref[nlead + 1 : nlead + 2, here] - used) / total


def finish(regions, summed, traits, nlead, nregion, total):
    chunk = summed.shape[1] - nregion * nlead
    return pl.pallas_call(
        functools.partial(finish_kernel, traits, total),
        in_specs=[
            pl.BlockSpec(memory_space=pltpu.SMEM),
            pl.BlockSpec(memory_space=pltpu.VMEM),
        ],
        out_specs=pl.BlockSpec(memory_space=pltpu.VMEM),
        out_shape=jax.ShapeDtypeStruct((8, chunk), jnp.float32),
        scratch_shapes=[
            pltpu.VMEM((nregion, nlead, nlead), jnp.float32),
            pltpu.VMEM((nregion, nlead, VB), jnp.float32),
            pltpu.VMEM((nregion, nlead, VB), jnp.float32),
        ],
        name="conditional_finish",
    )(regions, summed)


def body(genotypes, residuals, weights, block_regions, leads):
    samples, local_vars = genotypes.shape
    nvar = lax.axis_size("var")
    nsamp = lax.axis_size("samp")
    myself = lax.axis_index("var")
    nregion = leads.shape[0] // nvar
    nlead = leads.shape[1]
    traits = residuals.shape[1]
    nchunk = nsamp // traits
    slots = nregion * nlead
    total = samples * nsamp
    listed = leads.reshape(nvar, slots)
    outgoing = gather(listed, genotypes)
    incoming = lax.all_to_all(outgoing, "var", split_axis=0, concat_axis=0, tiled=True)
    mine = lax.dynamic_index_in_dim(listed, myself, 0, keepdims=False)
    source = mine // local_vars
    order = jnp.arange(slots, dtype=jnp.int32)
    earlier = (source[:, None] == source[None, :]) & (order[None, :] < order[:, None])
    slot = source[:, None] * HOST + jnp.sum(earlier.astype(jnp.int32), axis=1, keepdims=True)
    pad = jnp.zeros((EXTRA - traits, samples), jnp.bfloat16)
    side = jnp.concatenate([residuals.T, pad, weights.T, pad], axis=0)
    partial = cross_products(
        block_regions, slot, incoming, side, genotypes, traits, nregion, nchunk
    )
    partial = partial.reshape((nsamp,) + partial.shape[2:])
    summed = lax.psum_scatter(partial, "samp", scatter_dimension=0, tiled=False)
    result = finish(block_regions, summed, traits, nlead, nregion, total)
    shared = lax.all_gather(result[:2], "samp", axis=0, tiled=False)
    shared = shared.reshape(nchunk, traits, 2, local_vars // nchunk)
    shared = jnp.transpose(shared, (2, 1, 0, 3)).reshape(2, traits, local_vars)
    return (shared[0], shared[1])


def solution(mesh):
    in_specs = (P("samp", "var"), P("samp", None), P("samp", None), P("var"), P())
    out_specs = (P(None, "var"), P(None, "var"))
    return jax.shard_map(body, mesh=mesh, in_specs=in_specs, out_specs=out_specs, check_vma=False)
```

```python
import functools
import math

import jax
import jax.numpy as jnp
from jax import lax
from jax.experimental import pallas as pl
from jax.experimental.pallas import tpu as pltpu
from jax.sharding import PartitionSpec as P

VB = 128
HOST = 32
NT = (((1,), (1,)), ((), ()))
NN = (((1,), (0,)), ((), ()))
EXTRA = 16


def gather_kernel(listed_ref, geno_ref, out_ref, onehot):
    nvar, slots = listed_ref.shape
    local_vars = geno_ref.shape[1]

    @pl.when(pl.program_id(0) == 0)
    def _():
        base = lax.axis_index("var") * local_vars
        offset = listed_ref[...] - base
        hosted = (offset >= 0) & (offset < local_vars)
        before = lax.broadcasted_iota(jnp.int32, (slots, slots), 0) < lax.broadcasted_iota(
            jnp.int32, (slots, slots), 1
        )
        rank = lax.dot_general(
            hosted.astype(jnp.float32),
            before.astype(jnp.float32),
            NN,
            preferred_element_type=jnp.float32,
        ).astype(jnp.int32)
        rank = jnp.where(hosted, rank, HOST)
        place = lax.broadcasted_iota(jnp.int32, (HOST, slots), 0)
        lanes = lax.broadcasted_iota(jnp.int32, (HOST, local_vars), 1)
        for owner in range(nvar):
            match = rank[owner : owner + 1, :] == place
            picked = jnp.sum(
                jnp.where(match, offset[owner : owner + 1, :], 0), axis=1, keepdims=True
            )
            onehot[owner * HOST : (owner + 1) * HOST, :] = (
                (lanes == picked).astype(jnp.float32).astype(jnp.bfloat16)
            )

    out_ref[...] = lax.dot_general(
        onehot[...], geno_ref[...], NT, preferred_element_type=jnp.float32
    ).astype(jnp.bfloat16)


def gather(listed, genotypes, tile=256):
    samples, local_vars = genotypes.shape
    nvar, slots = listed.shape
    rows = nvar * HOST
    return pl.pallas_call(
        gather_kernel,
        grid=(samples // tile,),
        in_specs=[
            pl.BlockSpec((nvar, slots), lambda i: (0, 0)),
            pl.BlockSpec((tile, local_vars), lambda i: (i, 0)),
        ],
        out_specs=pl.BlockSpec((rows, tile), lambda i: (0, i)),
        out_shape=jax.ShapeDtypeStruct((rows, samples), jnp.bfloat16),
        scratch_shapes=[pltpu.VMEM((rows, local_vars), jnp.bfloat16)],
        name="lead_gather",
    )(listed, genotypes)


def cross_kernel(
    region_ref,
    slot_ref,
    incoming_ref,
    side_ref,
    geno_ref,
    cross_ref,
    small_ref,
    gram_ref,
    lead,
    weighted,
):
    nregion, rows, samples = weighted.shape
    nlead = lead.shape[0] // nregion
    traits = (rows - EXTRA) // nlead
    chunk = geno_ref.shape[1]
    step = pl.program_id(0)

    @pl.when(step == 0)
    def _():
        slots = incoming_ref.shape[0]
        pick = (
            lax.broadcasted_iota(jnp.int32, (nregion * nlead, slots), 1) == slot_ref[...]
        ).astype(jnp.float32).astype(jnp.bfloat16)
        lead[...] = lax.dot_general(
            pick, incoming_ref[...], NN, preferred_element_type=jnp.float32
        ).astype(jnp.bfloat16)
        for region in range(nregion):
            cols = lead[region * nlead : (region + 1) * nlead, :].astype(jnp.float32)
            for trait in range(traits):
                scale = side_ref[EXTRA + trait : EXTRA + trait + 1, :].astype(jnp.float32)
                weighted[region, trait * nlead : (trait + 1) * nlead, :] = (cols * scale).astype(
                    jnp.bfloat16
                )
            weighted[region, traits * nlead :, :] = side_ref[:EXTRA, :]
            gram = lax.dot_general(
                weighted[region],
                lead[region * nlead : (region + 1) * nlead, :],
                NT,
                preferred_element_type=jnp.float32,
            )
            there = slice(region * nlead, (region + 1) * nlead)
            last = traits * nlead
            for trait in range(traits):
                gram_ref[trait, :nlead, there] = gram[trait * nlead : (trait + 1) * nlead, :]
                gram_ref[trait, nlead : nlead + 1, there] = gram[last + trait : last + trait + 1, :]
                gram_ref[trait, nlead + 1 :, there] = jnp.zeros((7, nlead), jnp.float32)

    per_chunk = chunk // VB
    small_ref[...] = jnp.zeros_like(small_ref)
    for block in range(per_chunk):
        region = region_ref[step * per_chunk + block]
        cols = geno_ref[:, block * VB : (block + 1) * VB]
        acc = lax.dot_general(weighted[region], cols, NN, preferred_element_type=jnp.float32)
        square = cols.astype(jnp.float32)
        square = (square * square).astype(jnp.bfloat16)
        diag = lax.dot_general(
            side_ref[EXTRA:, :], square, NN, preferred_element_type=jnp.float32
        )
        here = slice(block * VB, (block + 1) * VB)
        last = traits * nlead
        other = per_chunk + block
        for trait in range(traits):
            cross_ref[trait, 0, :, here] = acc[trait * nlead : (trait + 1) * nlead, :].astype(
                jnp.bfloat16
            )
            small_ref[trait, 0, block : block + 1, :] = acc[last + trait : last + trait + 1, :]
            small_ref[trait, 0, other : other + 1, :] = diag[trait : trait + 1, :]


def cross_products(regions, slot, incoming, side, genotypes, traits, nregion, nchunk):
    samples, local_vars = genotypes.shape
    nlead = slot.shape[0] // nregion
    chunk = local_vars // nchunk
    rows = traits * nlead + EXTRA
    whole = lambda i, r: (0, 0)
    return pl.pallas_call(
        cross_kernel,
        grid_spec=pltpu.PrefetchScalarGridSpec(
            num_scalar_prefetch=1,
            grid=(nchunk,),
            in_specs=[
                pl.BlockSpec(slot.shape, whole),
                pl.BlockSpec(incoming.shape, whole),
                pl.BlockSpec(side.shape, whole),
                pl.BlockSpec((samples, chunk), lambda i, r: (0, i)),
            ],
            out_specs=[
                pl.BlockSpec((traits, 1, nlead, chunk), lambda i, r: (0, i, 0, 0)),
                pl.BlockSpec((traits, 1, 8, VB), lambda i, r: (0, i, 0, 0)),
                pl.BlockSpec((traits, nlead + 8, nregion * nlead), lambda i, r: (0, 0, 0)),
            ],
            scratch_shapes=[
                pltpu.VMEM((nregion * nlead, samples), jnp.bfloat16),
                pltpu.VMEM((nregion, rows, samples), jnp.bfloat16),
            ],
        ),
        out_shape=[
            jax.ShapeDtypeStruct((traits, nchunk, nlead, chunk), jnp.bfloat16),
            jax.ShapeDtypeStruct((traits, nchunk, 8, VB), jnp.float32),
            jax.ShapeDtypeStruct((traits, nlead + 8, nregion * nlead), jnp.float32),
        ],
        compiler_params=pltpu.CompilerParams(vmem_limit_bytes=48 * 1024 * 1024),
        name="cross_products",
    )(regions, slot, incoming, side, genotypes)


def meet(peers):
    barrier = pltpu.get_barrier_semaphore()
    for peer in peers:
        pl.semaphore_signal(
            barrier, inc=1, device_id={"samp": peer}, device_id_type=pl.DeviceIdType.MESH
        )
    pl.semaphore_wait(barrier, len(peers))


def places(nx, nz):
    me = lax.axis_index("samp")
    x, z = lax.rem(me, nx), lax.div(me, nx)
    xpeers = [z * nx + lax.rem(x + d, nx) for d in range(1, nx)]
    zpeers = [lax.rem(z + d, nz) * nx + x for d in range(1, nz)]
    return x, z, xpeers, zpeers


def reduce_kernel(
    cross_ref,
    small_ref,
    gram_ref,
    cross_out,
    small_out,
    gram_out,
    x_cross,
    x_small,
    x_gram,
    mid_cross,
    mid_small,
    mid_gram,
    z_cross,
    z_small,
    z_gram,
    sent,
    got,
):
    nx, nz = cross_ref.shape[:2]
    x, z, xpeers, zpeers = places(nx, nz)
    meet(xpeers + zpeers)
    started = []

    def push(source, target, peer):
        count = len(started)
        copy = pltpu.make_async_remote_copy(
            src_ref=source,
            dst_ref=target,
            send_sem=sent.at[count],
            recv_sem=got.at[count],
            device_id={"samp": peer},
            device_id_type=pl.DeviceIdType.MESH,
        )
        copy.start()
        started.append(copy)
        return copy

    order = sorted(range(1, nz), key=lambda d: -min(d, nz - d)) + [0]
    early = []
    for i, peer in enumerate(xpeers):
        trait = lax.rem(x + i + 1, nx)
        early.append(push(gram_ref.at[trait], x_gram.at[i], peer))
        early.append(push(small_ref.at[trait], x_small.at[i], peer))
    chunks = {}
    for d in order:
        chunk = lax.rem(z + d, nz)
        chunks[d] = [
            push(cross_ref.at[lax.rem(x + i + 1, nx), chunk], x_cross.at[i, d], peer)
            for i, peer in enumerate(xpeers)
        ]
    for copy in early:
        copy.wait_recv()
    mid_gram[...] = gram_ref[x] + x_gram[0] + x_gram[1] + x_gram[2]
    mid_small[...] = small_ref[x] + x_small[0] + x_small[1] + x_small[2]
    late = []
    for d in order:
        chunk = lax.rem(z + d, nz)
        if d > 0:
            peer = zpeers[d - 1]
            late.append(push(mid_gram, z_gram.at[d - 1], peer))
            late.append(push(mid_small.at[chunk], z_small.at[d - 1], peer))
        for copy in chunks[d]:
            copy.wait_recv()
        total = cross_ref[x, chunk].astype(jnp.float32)
        for i in range(nx - 1):
            total = total + x_cross[i, d].astype(jnp.float32)
        if d > 0:
            mid_cross[d] = total.astype(jnp.bfloat16)
            late.append(push(mid_cross.at[d], z_cross.at[d - 1], zpeers[d - 1]))
        else:
            cross_out[...] = total
    for copy in late:
        copy.wait_recv()
    gram = mid_gram[...]
    small = mid_small[z]
    cross = cross_out[...]
    for d in range(nz - 1):
        gram = gram + z_gram[d]
        small = small + z_small[d]
        cross = cross + z_cross[d].astype(jnp.float32)
    gram_out[...] = gram
    small_out[...] = small
    cross_out[...] = cross
    for copy in started:
        copy.wait_send()


def reduce_over_samples(cross, small, gram):
    nx, nz = cross.shape[:2]
    count = 2 * (nx - 1) + nz * (nx - 1) + 3 * (nz - 1)
    vmem = pl.BlockSpec(memory_space=pltpu.VMEM)
    lands = lambda lead, array, skip: pltpu.VMEM(lead + array.shape[skip:], array.dtype)
    return pl.pallas_call(
        reduce_kernel,
        in_specs=[vmem] * 3,
        out_specs=[vmem] * 3,
        out_shape=[
            jax.ShapeDtypeStruct(cross.shape[2:], jnp.float32),
            jax.ShapeDtypeStruct(small.shape[2:], jnp.float32),
            jax.ShapeDtypeStruct(gram.shape[1:], jnp.float32),
        ],
        scratch_shapes=[
            lands((nx - 1, nz), cross, 2),
            lands((nx - 1, nz), small, 2),
            lands((nx - 1,), gram, 1),
            lands((nz,), cross, 2),
            lands((nz,), small, 2),
            lands((), gram, 1),
            lands((nz - 1,), cross, 2),
            lands((nz - 1,), small, 2),
            lands((nz - 1,), gram, 1),
            pltpu.SemaphoreType.DMA((count,)),
            pltpu.SemaphoreType.DMA((count,)),
        ],
        compiler_params=pltpu.CompilerParams(collective_id=0, has_side_effects=True),
        name="reduce_over_samples",
    )(cross, small, gram)


def share_kernel(nx, nz, result_ref, scores_ref, variances_ref, lane, whole, sent, got, here_sem):
    x, z, xpeers, zpeers = places(nx, nz)
    meet(xpeers + zpeers)
    own = pltpu.make_async_copy(result_ref, lane.at[z], here_sem.at[0])
    own.start()
    first = []
    for i, peer in enumerate(zpeers):
        copy = pltpu.make_async_remote_copy(
            src_ref=result_ref,
            dst_ref=lane.at[z],
            send_sem=sent.at[i],
            recv_sem=got.at[i],
            device_id={"samp": peer},
            device_id_type=pl.DeviceIdType.MESH,
        )
        copy.start()
        first.append(copy)
    own.wait()
    for copy in first:
        copy.wait_recv()
    mine = pltpu.make_async_copy(lane, whole.at[x], here_sem.at[1])
    mine.start()
    second = []
    for i, peer in enumerate(xpeers):
        copy = pltpu.make_async_remote_copy(
            src_ref=lane,
            dst_ref=whole.at[x],
            send_sem=sent.at[nz - 1 + i],
            recv_sem=got.at[nz - 1 + i],
            device_id={"samp": peer},
            device_id_type=pl.DeviceIdType.MESH,
        )
        copy.start()
        second.append(copy)
    mine.wait()
    for copy in second:
        copy.wait_recv()
    per_chunk = scores_ref.shape[1] // (nz * VB)
    for trait in range(nx):
        for chunk in range(nz):
            tile = whole[trait, chunk]
            for block in range(per_chunk):
                at = (chunk * per_chunk + block) * VB
                scores_ref[trait : trait + 1, at : at + VB] = tile[block : block + 1, :]
                variances_ref[trait : trait + 1, at : at + VB] = tile[
                    per_chunk + block : per_chunk + block + 1, :
                ]
    for copy in first + second:
        copy.wait_send()


def share(result, nx, nz, local_vars):
    vmem = pl.BlockSpec(memory_space=pltpu.VMEM)
    out = jax.ShapeDtypeStruct((nx, local_vars), jnp.float32)
    count = nx + nz - 2
    return pl.pallas_call(
        functools.partial(share_kernel, nx, nz),
        in_specs=[vmem],
        out_specs=[vmem] * 2,
        out_shape=[out, out],
        scratch_shapes=[
            pltpu.VMEM((nz,) + result.shape, jnp.float32),
            pltpu.VMEM((nx, nz) + result.shape, jnp.float32),
            pltpu.SemaphoreType.DMA((count,)),
            pltpu.SemaphoreType.DMA((count,)),
            pltpu.SemaphoreType.DMA((2,)),
        ],
        compiler_params=pltpu.CompilerParams(collective_id=1, has_side_effects=True),
        name="share_results",
    )(result)


def finish_kernel(
    traits, total, region_ref, cross_ref, small_ref, gram_ref, out_ref, inverse, pivots, target
):
    nregion, nlead, _ = inverse.shape
    chunk = cross_ref.shape[1]
    per_chunk = chunk // VB
    first = (lax.axis_index("samp") // traits) * per_chunk
    eye = (
        lax.broadcasted_iota(jnp.int32, (nlead, nlead), 0)
        == lax.broadcasted_iota(jnp.int32, (nlead, nlead), 1)
    )
    unit = eye.astype(jnp.float32)
    below = lax.broadcasted_iota(jnp.int32, (nlead, 1), 0)
    state = [
        jnp.concatenate(
            [gram_ref[:nlead, r * nlead : (r + 1) * nlead], unit], axis=1
        )
        for r in range(nregion)
    ]
    for j in range(nlead - 1):
        for r in range(nregion):
            row = state[r][j : j + 1, :]
            ratio = state[r][:, j : j + 1] / row[:, j : j + 1]
            state[r] = state[r] - jnp.where(below > j, ratio, 0.0) * row
    for r in range(nregion):
        lower = state[r][:, nlead:]
        upper = state[r][:, :nlead]
        inverse[r] = lower
        pivot = 1.0 / jnp.sum(jnp.where(eye, upper, 0.0), axis=1, keepdims=True)
        score = gram_ref[nlead : nlead + 1, r * nlead : (r + 1) * nlead]
        pivots[r] = jnp.broadcast_to(pivot, (nlead, VB))
        target[r] = jnp.broadcast_to(
            jnp.sum(lower * score, axis=1, keepdims=True) * pivot, (nlead, VB)
        )
    out_ref[...] = jnp.zeros_like(out_ref)
    for block in range(per_chunk):
        here = slice(block * VB, (block + 1) * VB)
        region = region_ref[first + block]
        solved = lax.dot_general(
            inverse[region],
            cross_ref[:, here],
            NN,
            preferred_element_type=jnp.float32,
            precision=lax.Precision.HIGHEST,
        )
        fit = jnp.sum(solved * target[region], axis=0, keepdims=True)
        used = jnp.sum(solved * solved * pivots[region], axis=0, keepdims=True)
        other = per_chunk + block
        out_ref[block : block + 1, :] = (small_ref[block : block + 1, :] - fit) / math.sqrt(total)
        out_ref[other : other + 1, :] = (small_ref[other : other + 1, :] - used) / total


def finish(regions, cross, small, gram, traits, nlead, nregion, total):
    vmem = pl.BlockSpec(memory_space=pltpu.VMEM)
    return pl.pallas_call(
        functools.partial(finish_kernel, traits, total),
        in_specs=[
            pl.BlockSpec(memory_space=pltpu.SMEM),
            vmem,
            vmem,
            vmem,
        ],
        out_specs=pl.BlockSpec(memory_space=pltpu.VMEM),
        out_shape=jax.ShapeDtypeStruct(small.shape, jnp.float32),
        scratch_shapes=[
            pltpu.VMEM((nregion, nlead, nlead), jnp.float32),
            pltpu.VMEM((nregion, nlead, VB), jnp.float32),
            pltpu.VMEM((nregion, nlead, VB), jnp.float32),
        ],
        name="conditional_finish",
    )(regions, cross, small, gram)


def body(genotypes, residuals, weights, block_regions, leads):
    samples, local_vars = genotypes.shape
    nvar = lax.axis_size("var")
    nsamp = lax.axis_size("samp")
    myself = lax.axis_index("var")
    nregion = leads.shape[0] // nvar
    nlead = leads.shape[1]
    traits = residuals.shape[1]
    nchunk = nsamp // traits
    slots = nregion * nlead
    total = samples * nsamp
    listed = leads.reshape(nvar, slots)
    outgoing = gather(listed, genotypes)
    incoming = lax.all_to_all(outgoing, "var", split_axis=0, concat_axis=0, tiled=True)
    mine = lax.dynamic_index_in_dim(listed, myself, 0, keepdims=False)
    source = mine // local_vars
    order = jnp.arange(slots, dtype=jnp.int32)
    earlier = (source[:, None] == source[None, :]) & (order[None, :] < order[:, None])
    slot = source[:, None] * HOST + jnp.sum(earlier.astype(jnp.int32), axis=1, keepdims=True)
    pad = jnp.zeros((EXTRA - traits, samples), jnp.bfloat16)
    side = jnp.concatenate([residuals.T, pad, weights.T, pad], axis=0)
    partial = cross_products(
        block_regions, slot, incoming, side, genotypes, traits, nregion, nchunk
    )
    cross, small, gram = reduce_over_samples(*partial)
    result = finish(block_regions, cross, small, gram, traits, nlead, nregion, total)
    scores, variances = share(result, traits, nchunk, local_vars)
    return (scores, variances)


def solution(mesh):
    in_specs = (P("samp", "var"), P("samp", None), P("samp", None), P("var"), P())
    out_specs = (P(None, "var"), P(None, "var"))
    return jax.shard_map(body, mesh=mesh, in_specs=in_specs, out_specs=out_specs, check_vma=False)
```

```python
import functools
import math

import jax
import jax.numpy as jnp
from jax import lax
from jax.experimental import pallas as pl
from jax.experimental.pallas import tpu as pltpu
from jax.sharding import PartitionSpec as P

VB = 128
HOST = 32
NT = (((1,), (1,)), ((), ()))
NN = (((1,), (0,)), ((), ()))
EXTRA = 16


def greet(axis, peers):
    barrier = pltpu.get_barrier_semaphore()
    for peer in peers:
        pl.semaphore_signal(
            barrier, inc=1, device_id={axis: peer}, device_id_type=pl.DeviceIdType.MESH
        )


def hear(peers):
    pl.semaphore_wait(pltpu.get_barrier_semaphore(), len(peers))


def meet(peers):
    greet("samp", peers)
    hear(peers)


def gather_kernel(listed_ref, geno_ref, out_ref, onehot, leaving, landed, sent, got):
    nvar, slots = listed_ref.shape
    local_vars = geno_ref.shape[1]
    tile = geno_ref.shape[0]
    ntile = leaving.shape[0]
    step = pl.program_id(0)
    me = lax.axis_index("var")
    peers = [lax.rem(me + d, nvar) for d in range(1, nvar)]

    @pl.when(step == 0)
    def _():
        greet("var", peers)
        base = me * local_vars
        offset = listed_ref[...] - base
        hosted = (offset >= 0) & (offset < local_vars)
        before = lax.broadcasted_iota(jnp.int32, (slots, slots), 0) < lax.broadcasted_iota(
            jnp.int32, (slots, slots), 1
        )
        rank = lax.dot_general(
            hosted.astype(jnp.float32),
            before.astype(jnp.float32),
            NN,
            preferred_element_type=jnp.float32,
        ).astype(jnp.int32)
        rank = jnp.where(hosted, rank, HOST)
        place = lax.broadcasted_iota(jnp.int32, (HOST, slots), 0)
        lanes = lax.broadcasted_iota(jnp.int32, (HOST, local_vars), 1)
        for owner in range(nvar):
            match = rank[owner : owner + 1, :] == place
            picked = jnp.sum(
                jnp.where(match, offset[owner : owner + 1, :], 0), axis=1, keepdims=True
            )
            onehot[owner * HOST : (owner + 1) * HOST, :] = (
                (lanes == picked).astype(jnp.float32).astype(jnp.bfloat16)
            )
        hear(peers)

    found = lax.dot_general(
        onehot[...], geno_ref[...], NT, preferred_element_type=jnp.float32
    ).astype(jnp.bfloat16)
    for owner in range(nvar):
        leaving[step, owner] = found[owner * HOST : (owner + 1) * HOST, :]

    def copy_to(turn, i):
        return pltpu.make_async_remote_copy(
            src_ref=leaving.at[turn, peers[i]],
            dst_ref=landed.at[turn, i],
            send_sem=sent.at[turn, i],
            recv_sem=got.at[turn, i],
            device_id={"var": peers[i]},
            device_id_type=pl.DeviceIdType.MESH,
        )

    for i in range(nvar - 1):
        copy_to(step, i).start()

    @pl.when(step == ntile - 1)
    def _():
        for turn in range(ntile):
            at = slice(turn * tile, (turn + 1) * tile)
            out_ref[me, :, at] = leaving[turn, me]
            for i in range(nvar - 1):
                copy_to(turn, i).wait_recv()
                out_ref[lax.rem(me + nvar - 1 - i, nvar), :, at] = landed[turn, i]
        for turn in range(ntile):
            for i in range(nvar - 1):
                copy_to(turn, i).wait_send()


def gather(listed, genotypes, tile=256):
    samples, local_vars = genotypes.shape
    nvar, slots = listed.shape
    rows = nvar * HOST
    ntile = samples // tile
    found = pl.pallas_call(
        gather_kernel,
        grid=(ntile,),
        in_specs=[
            pl.BlockSpec((nvar, slots), lambda i: (0, 0)),
            pl.BlockSpec((tile, local_vars), lambda i: (i, 0)),
        ],
        out_specs=pl.BlockSpec((nvar, HOST, samples), lambda i: (0, 0, 0)),
        out_shape=jax.ShapeDtypeStruct((nvar, HOST, samples), jnp.bfloat16),
        scratch_shapes=[
            pltpu.VMEM((rows, local_vars), jnp.bfloat16),
            pltpu.VMEM((ntile, nvar, HOST, tile), jnp.bfloat16),
            pltpu.VMEM((ntile, nvar - 1, HOST, tile), jnp.bfloat16),
            pltpu.SemaphoreType.DMA((ntile, nvar - 1)),
            pltpu.SemaphoreType.DMA((ntile, nvar - 1)),
        ],
        compiler_params=pltpu.CompilerParams(collective_id=2, has_side_effects=True),
        name="lead_exchange",
    )(listed, genotypes)
    return found.reshape(rows, samples)


def places(nx, nz):
    me = lax.axis_index("samp")
    x, z = lax.rem(me, nx), lax.div(me, nx)
    xpeers = [z * nx + lax.rem(x + d, nx) for d in range(1, nx)]
    zpeers = [lax.rem(z + d, nz) * nx + x for d in range(1, nz)]
    return x, z, xpeers, zpeers


def reduce_kernel(
    region_ref,
    slot_ref,
    incoming_ref,
    side_ref,
    geno_ref,
    cross_out,
    small_out,
    gram_out,
    lead,
    weighted,
    cols_buf,
    cross_own,
    small_own,
    gram_own,
    x_cross,
    x_small,
    x_gram,
    mid_cross,
    mid_small,
    mid_gram,
    z_cross,
    z_small,
    z_gram,
    fetched,
    sent_x,
    got_x,
    sent_z,
    got_z,
):
    nx, nz = cross_own.shape[:2]
    nregion, rows, samples = weighted.shape
    nlead = lead.shape[0] // nregion
    chunk_cols = cols_buf.shape[2]
    per_chunk = chunk_cols // VB
    last = nx * nlead
    x, z, xpeers, zpeers = places(nx, nz)
    greet("samp", xpeers + zpeers)

    def turn_of(step):
        turn = lax.rem(step + nz // 2, nz)
        return turn, lax.rem(z + turn, nz)

    def fetch(step):
        chunk = turn_of(step)[1]
        start = pl.multiple_of(chunk * chunk_cols, VB)
        slot = lax.rem(step, 2)
        return pltpu.make_async_copy(
            geno_ref.at[:, pl.ds(start, chunk_cols)], cols_buf.at[slot], fetched.at[slot]
        )

    def remote(source, target, sent, got, peer):
        return pltpu.make_async_remote_copy(
            src_ref=source,
            dst_ref=target,
            send_sem=sent,
            recv_sem=got,
            device_id={"samp": peer},
            device_id_type=pl.DeviceIdType.MESH,
        )

    def x_copies(i, turn):
        trait = lax.rem(x + i + 1, nx)
        return [
            remote(
                cross_own.at[trait, turn],
                x_cross.at[i, turn],
                sent_x.at[0, i, turn],
                got_x.at[0, i, turn],
                xpeers[i],
            ),
            remote(
                small_own.at[trait, turn],
                x_small.at[i, turn],
                sent_x.at[1, i, turn],
                got_x.at[1, i, turn],
                xpeers[i],
            ),
        ]

    def x_gram_copy(i):
        trait = lax.rem(x + i + 1, nx)
        return remote(
            gram_own.at[trait], x_gram.at[i], sent_x.at[0, i, nz], got_x.at[0, i, nz], xpeers[i]
        )

    def z_copies(turn):
        peer = lax.rem(z + turn, nz) * nx + x
        return [
            remote(
                mid_cross.at[turn], z_cross.at[turn], sent_z.at[0, turn], got_z.at[0, turn], peer
            ),
            remote(
                mid_small.at[turn], z_small.at[turn], sent_z.at[1, turn], got_z.at[1, turn], peer
            ),
        ]

    def z_gram_copy(d):
        return remote(
            mid_gram, z_gram.at[d], sent_z.at[2, d], got_z.at[2, d], zpeers[d - 1]
        )

    fetch(0).start()
    slots = incoming_ref.shape[0]
    pick = (
        lax.broadcasted_iota(jnp.int32, (nregion * nlead, slots), 1) == slot_ref[...]
    ).astype(jnp.float32).astype(jnp.bfloat16)
    lead[...] = lax.dot_general(
        pick, incoming_ref[...], NN, preferred_element_type=jnp.float32
    ).astype(jnp.bfloat16)
    for region in range(nregion):
        cols = lead[region * nlead : (region + 1) * nlead, :].astype(jnp.float32)
        for trait in range(nx):
            scale = side_ref[EXTRA + trait : EXTRA + trait + 1, :].astype(jnp.float32)
            weighted[region, trait * nlead : (trait + 1) * nlead, :] = (cols * scale).astype(
                jnp.bfloat16
            )
        weighted[region, last:, :] = side_ref[:EXTRA, :]
        gram = lax.dot_general(
            weighted[region],
            lead[region * nlead : (region + 1) * nlead, :],
            NT,
            preferred_element_type=jnp.float32,
        )
        there = slice(region * nlead, (region + 1) * nlead)
        for trait in range(nx):
            gram_own[trait, :nlead, there] = gram[trait * nlead : (trait + 1) * nlead, :]
            gram_own[trait, nlead : nlead + 1, there] = gram[last + trait : last + trait + 1, :]
            gram_own[trait, nlead + 1 :, there] = jnp.zeros((7, nlead), jnp.float32)
    small_own[...] = jnp.zeros_like(small_own)
    hear(xpeers + zpeers)
    for i in range(nx - 1):
        x_gram_copy(i).start()

    def multiply(step, carry):
        turn, chunk = turn_of(step)
        slot = lax.rem(step, 2)
        fetch(step).wait()

        @pl.when(step < nz - 1)
        def _():
            fetch(step + 1).start()

        for block in range(per_chunk):
            here = slice(block * VB, (block + 1) * VB)
            region = region_ref[chunk * per_chunk + block]
            cols = cols_buf[slot, :, here]
            acc = lax.dot_general(weighted[region], cols, NN, preferred_element_type=jnp.float32)
            square = cols.astype(jnp.float32)
            square = (square * square).astype(jnp.bfloat16)
            diag = lax.dot_general(
                side_ref[EXTRA:, :], square, NN, preferred_element_type=jnp.float32
            )
            other = per_chunk + block
            for trait in range(nx):
                cross_own[trait, turn, :, here] = acc[
                    trait * nlead : (trait + 1) * nlead, :
                ].astype(jnp.bfloat16)
                small_own[trait, turn, block : block + 1, :] = acc[
                    last + trait : last + trait + 1, :
                ]
                small_own[trait, turn, other : other + 1, :] = diag[trait : trait + 1, :]
        for i in range(nx - 1):
            for copy in x_copies(i, turn):
                copy.start()
        return carry

    lax.fori_loop(0, nz, multiply, 0)
    gram = gram_own[x]
    for i in range(nx - 1):
        x_gram_copy(i).wait_recv()
        gram = gram + x_gram[i]
    mid_gram[...] = gram
    for d in range(1, nz):
        z_gram_copy(d).start()

    def combine(step, carry):
        turn = turn_of(step)[0]
        cross = cross_own[x, turn].astype(jnp.float32)
        small = small_own[x, turn]
        for i in range(nx - 1):
            for copy in x_copies(i, turn):
                copy.wait_recv()
            cross = cross + x_cross[i, turn].astype(jnp.float32)
            small = small + x_small[i, turn]
        mid_small[turn] = small

        @pl.when(turn > 0)
        def _():
            mid_cross[turn] = cross.astype(jnp.bfloat16)
            for copy in z_copies(turn):
                copy.start()

        @pl.when(turn == 0)
        def _():
            cross_out[...] = cross

        return carry

    lax.fori_loop(0, nz, combine, 0)
    gram = mid_gram[...]
    small = mid_small[0]
    cross = cross_out[...]
    for d in range(1, nz):
        z_gram_copy(d).wait_recv()
        for copy in z_copies(d):
            copy.wait_recv()
        gram = gram + z_gram[d]
        small = small + z_small[d]
        cross = cross + z_cross[d].astype(jnp.float32)
    gram_out[...] = gram
    small_out[...] = small
    cross_out[...] = cross
    for i in range(nx - 1):
        x_gram_copy(i).wait_send()
        for turn in range(nz):
            for copy in x_copies(i, turn):
                copy.wait_send()
    for d in range(1, nz):
        z_gram_copy(d).wait_send()
        for copy in z_copies(d):
            copy.wait_send()


def cross_products(regions, slot, incoming, side, genotypes, nx, nregion, nz):
    samples, local_vars = genotypes.shape
    nlead = slot.shape[0] // nregion
    chunk = local_vars // nz
    rows = nx * nlead + EXTRA
    vmem = pl.BlockSpec(memory_space=pltpu.VMEM)
    cross = lambda *lead: pltpu.VMEM(lead + (nlead, chunk), jnp.bfloat16)
    small = lambda *lead: pltpu.VMEM(lead + (8, VB), jnp.float32)
    gram = lambda *lead: pltpu.VMEM(lead + (nlead + 8, nregion * nlead), jnp.float32)
    return pl.pallas_call(
        reduce_kernel,
        in_specs=[
            pl.BlockSpec(memory_space=pltpu.SMEM),
            vmem,
            vmem,
            vmem,
            pl.BlockSpec(memory_space=pl.ANY),
        ],
        out_specs=[vmem] * 3,
        out_shape=[
            jax.ShapeDtypeStruct((nlead, chunk), jnp.float32),
            jax.ShapeDtypeStruct((8, VB), jnp.float32),
            jax.ShapeDtypeStruct((nlead + 8, nregion * nlead), jnp.float32),
        ],
        scratch_shapes=[
            pltpu.VMEM((nregion * nlead, samples), jnp.bfloat16),
            pltpu.VMEM((nregion, rows, samples), jnp.bfloat16),
            pltpu.VMEM((2, samples, chunk), jnp.bfloat16),
            cross(nx, nz),
            small(nx, nz),
            gram(nx),
            cross(nx - 1, nz),
            small(nx - 1, nz),
            gram(nx - 1),
            cross(nz),
            small(nz),
            gram(),
            cross(nz),
            small(nz),
            gram(nz),
            pltpu.SemaphoreType.DMA((2,)),
            pltpu.SemaphoreType.DMA((2, nx - 1, nz + 1)),
            pltpu.SemaphoreType.DMA((2, nx - 1, nz + 1)),
            pltpu.SemaphoreType.DMA((3, nz)),
            pltpu.SemaphoreType.DMA((3, nz)),
        ],
        compiler_params=pltpu.CompilerParams(
            collective_id=0, has_side_effects=True, vmem_limit_bytes=48 * 1024 * 1024
        ),
        name="cross_and_reduce",
    )(regions, slot, incoming, side, genotypes)


def share_kernel(nx, nz, result_ref, scores_ref, variances_ref, lane, whole, sent, got, here_sem):
    x, z, xpeers, zpeers = places(nx, nz)
    meet(xpeers + zpeers)
    own = pltpu.make_async_copy(result_ref, lane.at[z], here_sem.at[0])
    own.start()
    first = []
    for i, peer in enumerate(zpeers):
        copy = pltpu.make_async_remote_copy(
            src_ref=result_ref,
            dst_ref=lane.at[z],
            send_sem=sent.at[i],
            recv_sem=got.at[i],
            device_id={"samp": peer},
            device_id_type=pl.DeviceIdType.MESH,
        )
        copy.start()
        first.append(copy)
    own.wait()
    for copy in first:
        copy.wait_recv()
    mine = pltpu.make_async_copy(lane, whole.at[x], here_sem.at[1])
    mine.start()
    second = []
    for i, peer in enumerate(xpeers):
        copy = pltpu.make_async_remote_copy(
            src_ref=lane,
            dst_ref=whole.at[x],
            send_sem=sent.at[nz - 1 + i],
            recv_sem=got.at[nz - 1 + i],
            device_id={"samp": peer},
            device_id_type=pl.DeviceIdType.MESH,
        )
        copy.start()
        second.append(copy)
    mine.wait()
    for copy in second:
        copy.wait_recv()
    per_chunk = scores_ref.shape[1] // (nz * VB)
    for trait in range(nx):
        for chunk in range(nz):
            tile = whole[trait, chunk]
            for block in range(per_chunk):
                at = (chunk * per_chunk + block) * VB
                scores_ref[trait : trait + 1, at : at + VB] = tile[block : block + 1, :]
                variances_ref[trait : trait + 1, at : at + VB] = tile[
                    per_chunk + block : per_chunk + block + 1, :
                ]
    for copy in first + second:
        copy.wait_send()


def share(result, nx, nz, local_vars):
    vmem = pl.BlockSpec(memory_space=pltpu.VMEM)
    out = jax.ShapeDtypeStruct((nx, local_vars), jnp.float32)
    count = nx + nz - 2
    return pl.pallas_call(
        functools.partial(share_kernel, nx, nz),
        in_specs=[vmem],
        out_specs=[vmem] * 2,
        out_shape=[out, out],
        scratch_shapes=[
            pltpu.VMEM((nz,) + result.shape, jnp.float32),
            pltpu.VMEM((nx, nz) + result.shape, jnp.float32),
            pltpu.SemaphoreType.DMA((count,)),
            pltpu.SemaphoreType.DMA((count,)),
            pltpu.SemaphoreType.DMA((2,)),
        ],
        compiler_params=pltpu.CompilerParams(collective_id=1, has_side_effects=True),
        name="share_results",
    )(result)


def finish_kernel(
    traits, total, region_ref, cross_ref, small_ref, gram_ref, out_ref, inverse, pivots, target
):
    nregion, nlead, _ = inverse.shape
    chunk = cross_ref.shape[1]
    per_chunk = chunk // VB
    first = (lax.axis_index("samp") // traits) * per_chunk
    eye = (
        lax.broadcasted_iota(jnp.int32, (nlead, nlead), 0)
        == lax.broadcasted_iota(jnp.int32, (nlead, nlead), 1)
    )
    unit = eye.astype(jnp.float32)
    below = lax.broadcasted_iota(jnp.int32, (nlead, 1), 0)
    state = [
        jnp.concatenate(
            [gram_ref[:nlead, r * nlead : (r + 1) * nlead], unit], axis=1
        )
        for r in range(nregion)
    ]
    for j in range(nlead - 1):
        for r in range(nregion):
            row = state[r][j : j + 1, :]
            ratio = state[r][:, j : j + 1] / row[:, j : j + 1]
            state[r] = state[r] - jnp.where(below > j, ratio, 0.0) * row
    for r in range(nregion):
        lower = state[r][:, nlead:]
        upper = state[r][:, :nlead]
        inverse[r] = lower
        pivot = 1.0 / jnp.sum(jnp.where(eye, upper, 0.0), axis=1, keepdims=True)
        score = gram_ref[nlead : nlead + 1, r * nlead : (r + 1) * nlead]
        pivots[r] = jnp.broadcast_to(pivot, (nlead, VB))
        target[r] = jnp.broadcast_to(
            jnp.sum(lower * score, axis=1, keepdims=True) * pivot, (nlead, VB)
        )
    out_ref[...] = jnp.zeros_like(out_ref)
    for block in range(per_chunk):
        here = slice(block * VB, (block + 1) * VB)
        region = region_ref[first + block]
        solved = lax.dot_general(
            inverse[region],
            cross_ref[:, here],
            NN,
            preferred_element_type=jnp.float32,
            precision=lax.Precision.HIGHEST,
        )
        fit = jnp.sum(solved * target[region], axis=0, keepdims=True)
        used = jnp.sum(solved * solved * pivots[region], axis=0, keepdims=True)
        other = per_chunk + block
        out_ref[block : block + 1, :] = (small_ref[block : block + 1, :] - fit) / math.sqrt(total)
        out_ref[other : other + 1, :] = (small_ref[other : other + 1, :] - used) / total


def finish(regions, cross, small, gram, traits, nlead, nregion, total):
    vmem = pl.BlockSpec(memory_space=pltpu.VMEM)
    return pl.pallas_call(
        functools.partial(finish_kernel, traits, total),
        in_specs=[
            pl.BlockSpec(memory_space=pltpu.SMEM),
            vmem,
            vmem,
            vmem,
        ],
        out_specs=pl.BlockSpec(memory_space=pltpu.VMEM),
        out_shape=jax.ShapeDtypeStruct(small.shape, jnp.float32),
        scratch_shapes=[
            pltpu.VMEM((nregion, nlead, nlead), jnp.float32),
            pltpu.VMEM((nregion, nlead, VB), jnp.float32),
            pltpu.VMEM((nregion, nlead, VB), jnp.float32),
        ],
        name="conditional_finish",
    )(regions, cross, small, gram)


def body(genotypes, residuals, weights, block_regions, leads):
    samples, local_vars = genotypes.shape
    nvar = lax.axis_size("var")
    nsamp = lax.axis_size("samp")
    myself = lax.axis_index("var")
    nregion = leads.shape[0] // nvar
    nlead = leads.shape[1]
    traits = residuals.shape[1]
    nchunk = nsamp // traits
    slots = nregion * nlead
    total = samples * nsamp
    listed = leads.reshape(nvar, slots)
    incoming = gather(listed, genotypes)
    mine = lax.dynamic_index_in_dim(listed, myself, 0, keepdims=False)
    source = mine // local_vars
    order = jnp.arange(slots, dtype=jnp.int32)
    earlier = (source[:, None] == source[None, :]) & (order[None, :] < order[:, None])
    slot = source[:, None] * HOST + jnp.sum(earlier.astype(jnp.int32), axis=1, keepdims=True)
    pad = jnp.zeros((EXTRA - traits, samples), jnp.bfloat16)
    side = jnp.concatenate([residuals.T, pad, weights.T, pad], axis=0)
    cross, small, gram = cross_products(
        block_regions, slot, incoming, side, genotypes, traits, nregion, nchunk
    )
    result = finish(block_regions, cross, small, gram, traits, nlead, nregion, total)
    scores, variances = share(result, traits, nchunk, local_vars)
    return (scores, variances)


def solution(mesh):
    in_specs = (P("samp", "var"), P("samp", None), P("samp", None), P("var"), P())
    out_specs = (P(None, "var"), P(None, "var"))
    return jax.shard_map(body, mesh=mesh, in_specs=in_specs, out_specs=out_specs, check_vma=False)
```

```python
import functools
import math

import jax
import jax.numpy as jnp
from jax import lax
from jax.experimental import pallas as pl
from jax.experimental.pallas import tpu as pltpu
from jax.sharding import PartitionSpec as P

VB = 128
HOST = 32
NT = (((1,), (1,)), ((), ()))
NN = (((1,), (0,)), ((), ()))
EXTRA = 16


def greet(axis, peers):
    barrier = pltpu.get_barrier_semaphore()
    for peer in peers:
        pl.semaphore_signal(
            barrier, inc=1, device_id={axis: peer}, device_id_type=pl.DeviceIdType.MESH
        )


def hear(peers):
    pl.semaphore_wait(pltpu.get_barrier_semaphore(), len(peers))


def gather_kernel(listed_ref, geno_ref, out_ref, onehot, leaving, landed, sent, got):
    nvar, slots = listed_ref.shape
    local_vars = geno_ref.shape[1]
    tile = geno_ref.shape[0]
    ntile = leaving.shape[0]
    step = pl.program_id(0)
    me = lax.axis_index("var")
    peers = [lax.rem(me + d, nvar) for d in range(1, nvar)]

    @pl.when(step == 0)
    def _():
        greet("var", peers)
        base = me * local_vars
        offset = listed_ref[...] - base
        hosted = (offset >= 0) & (offset < local_vars)
        before = lax.broadcasted_iota(jnp.int32, (slots, slots), 0) < lax.broadcasted_iota(
            jnp.int32, (slots, slots), 1
        )
        rank = lax.dot_general(
            hosted.astype(jnp.float32),
            before.astype(jnp.float32),
            NN,
            preferred_element_type=jnp.float32,
        ).astype(jnp.int32)
        rank = jnp.where(hosted, rank, HOST)
        place = lax.broadcasted_iota(jnp.int32, (HOST, slots), 0)
        lanes = lax.broadcasted_iota(jnp.int32, (HOST, local_vars), 1)
        for owner in range(nvar):
            match = rank[owner : owner + 1, :] == place
            picked = jnp.sum(
                jnp.where(match, offset[owner : owner + 1, :], 0), axis=1, keepdims=True
            )
            onehot[owner * HOST : (owner + 1) * HOST, :] = (
                (lanes == picked).astype(jnp.float32).astype(jnp.bfloat16)
            )
        hear(peers)

    found = lax.dot_general(
        onehot[...], geno_ref[...], NT, preferred_element_type=jnp.float32
    ).astype(jnp.bfloat16)
    for owner in range(nvar):
        leaving[step, owner] = found[owner * HOST : (owner + 1) * HOST, :]

    def copy_to(turn, i):
        return pltpu.make_async_remote_copy(
            src_ref=leaving.at[turn, peers[i]],
            dst_ref=landed.at[turn, i],
            send_sem=sent.at[turn, i],
            recv_sem=got.at[turn, i],
            device_id={"var": peers[i]},
            device_id_type=pl.DeviceIdType.MESH,
        )

    for i in range(nvar - 1):
        copy_to(step, i).start()

    @pl.when(step == ntile - 1)
    def _():
        for turn in range(ntile):
            at = slice(turn * tile, (turn + 1) * tile)
            out_ref[me, :, at] = leaving[turn, me]
            for i in range(nvar - 1):
                copy_to(turn, i).wait_recv()
                out_ref[lax.rem(me + nvar - 1 - i, nvar), :, at] = landed[turn, i]
        for turn in range(ntile):
            for i in range(nvar - 1):
                copy_to(turn, i).wait_send()


def gather(listed, genotypes, tile=256):
    samples, local_vars = genotypes.shape
    nvar, slots = listed.shape
    rows = nvar * HOST
    ntile = samples // tile
    found = pl.pallas_call(
        gather_kernel,
        grid=(ntile,),
        in_specs=[
            pl.BlockSpec((nvar, slots), lambda i: (0, 0)),
            pl.BlockSpec((tile, local_vars), lambda i: (i, 0)),
        ],
        out_specs=pl.BlockSpec((nvar, HOST, samples), lambda i: (0, 0, 0)),
        out_shape=jax.ShapeDtypeStruct((nvar, HOST, samples), jnp.bfloat16),
        scratch_shapes=[
            pltpu.VMEM((rows, local_vars), jnp.bfloat16),
            pltpu.VMEM((ntile, nvar, HOST, tile), jnp.bfloat16),
            pltpu.VMEM((ntile, nvar - 1, HOST, tile), jnp.bfloat16),
            pltpu.SemaphoreType.DMA((ntile, nvar - 1)),
            pltpu.SemaphoreType.DMA((ntile, nvar - 1)),
        ],
        compiler_params=pltpu.CompilerParams(collective_id=2, has_side_effects=True),
        name="lead_exchange",
    )(listed, genotypes)
    return found.reshape(rows, samples)


def places(nx, nz):
    me = lax.axis_index("samp")
    x, z = lax.rem(me, nx), lax.div(me, nx)
    xpeers = [z * nx + lax.rem(x + d, nx) for d in range(1, nx)]
    zpeers = [lax.rem(z + d, nz) * nx + x for d in range(1, nz)]
    return x, z, xpeers, zpeers


def reduce_kernel(
    total,
    region_ref,
    slot_ref,
    incoming_ref,
    side_ref,
    geno_ref,
    scores_ref,
    variances_ref,
    lead,
    weighted,
    cols_buf,
    cross_own,
    small_own,
    gram_own,
    x_cross,
    x_small,
    x_gram,
    mid_cross,
    mid_small,
    mid_gram,
    z_cross,
    z_small,
    z_gram,
    cross_sum,
    inverse,
    pivots,
    target,
    result,
    lane,
    whole,
    fetched,
    sent_x,
    got_x,
    sent_z,
    got_z,
    sent_r,
    got_r,
):
    nx, nz = cross_own.shape[:2]
    nregion, rows, samples = weighted.shape
    nlead = lead.shape[0] // nregion
    chunk_cols = cols_buf.shape[2]
    per_chunk = chunk_cols // VB
    last = nx * nlead
    x, z, xpeers, zpeers = places(nx, nz)
    greet("samp", xpeers + zpeers)

    def turn_of(step):
        turn = lax.rem(step + nz // 2, nz)
        return turn, lax.rem(z + turn, nz)

    def fetch(step):
        chunk = turn_of(step)[1]
        start = pl.multiple_of(chunk * chunk_cols, VB)
        slot = lax.rem(step, 2)
        return pltpu.make_async_copy(
            geno_ref.at[:, pl.ds(start, chunk_cols)], cols_buf.at[slot], fetched.at[slot]
        )

    def remote(source, target, sent, got, peer):
        return pltpu.make_async_remote_copy(
            src_ref=source,
            dst_ref=target,
            send_sem=sent,
            recv_sem=got,
            device_id={"samp": peer},
            device_id_type=pl.DeviceIdType.MESH,
        )

    def x_copies(i, turn):
        trait = lax.rem(x + i + 1, nx)
        return [
            remote(
                cross_own.at[trait, turn],
                x_cross.at[i, turn],
                sent_x.at[0, i, turn],
                got_x.at[0, i, turn],
                xpeers[i],
            ),
            remote(
                small_own.at[trait, turn],
                x_small.at[i, turn],
                sent_x.at[1, i, turn],
                got_x.at[1, i, turn],
                xpeers[i],
            ),
        ]

    def x_gram_copy(i):
        trait = lax.rem(x + i + 1, nx)
        return remote(
            gram_own.at[trait], x_gram.at[i], sent_x.at[0, i, nz], got_x.at[0, i, nz], xpeers[i]
        )

    def z_copies(turn):
        peer = lax.rem(z + turn, nz) * nx + x
        return [
            remote(
                mid_cross.at[turn], z_cross.at[turn], sent_z.at[0, turn], got_z.at[0, turn], peer
            ),
            remote(
                mid_small.at[turn], z_small.at[turn], sent_z.at[1, turn], got_z.at[1, turn], peer
            ),
        ]

    def z_gram_copy(d):
        return remote(
            mid_gram, z_gram.at[d], sent_z.at[2, d], got_z.at[2, d], zpeers[d - 1]
        )

    fetch(0).start()
    slots = incoming_ref.shape[0]
    pick = (
        lax.broadcasted_iota(jnp.int32, (nregion * nlead, slots), 1) == slot_ref[...]
    ).astype(jnp.float32).astype(jnp.bfloat16)
    lead[...] = lax.dot_general(
        pick, incoming_ref[...], NN, preferred_element_type=jnp.float32
    ).astype(jnp.bfloat16)
    for region in range(nregion):
        cols = lead[region * nlead : (region + 1) * nlead, :].astype(jnp.float32)
        for trait in range(nx):
            scale = side_ref[EXTRA + trait : EXTRA + trait + 1, :].astype(jnp.float32)
            weighted[region, trait * nlead : (trait + 1) * nlead, :] = (cols * scale).astype(
                jnp.bfloat16
            )
        weighted[region, last:, :] = side_ref[:EXTRA, :]
        gram = lax.dot_general(
            weighted[region],
            lead[region * nlead : (region + 1) * nlead, :],
            NT,
            preferred_element_type=jnp.float32,
        )
        there = slice(region * nlead, (region + 1) * nlead)
        for trait in range(nx):
            gram_own[trait, :nlead, there] = gram[trait * nlead : (trait + 1) * nlead, :]
            gram_own[trait, nlead : nlead + 1, there] = gram[last + trait : last + trait + 1, :]
            gram_own[trait, nlead + 1 :, there] = jnp.zeros((7, nlead), jnp.float32)
    small_own[...] = jnp.zeros_like(small_own)
    hear(xpeers + zpeers)
    for i in range(nx - 1):
        x_gram_copy(i).start()

    def multiply(step, carry):
        turn, chunk = turn_of(step)
        slot = lax.rem(step, 2)
        fetch(step).wait()

        @pl.when(step < nz - 1)
        def _():
            fetch(step + 1).start()

        @pl.when(step == nz // 2)
        def _():
            gram = gram_own[x]
            for i in range(nx - 1):
                x_gram_copy(i).wait_recv()
                gram = gram + x_gram[i]
            mid_gram[...] = gram
            for d in range(1, nz):
                z_gram_copy(d).start()

        for block in range(per_chunk):
            here = slice(block * VB, (block + 1) * VB)
            region = region_ref[chunk * per_chunk + block]
            cols = cols_buf[slot, :, here]
            acc = lax.dot_general(weighted[region], cols, NN, preferred_element_type=jnp.float32)
            square = cols.astype(jnp.float32)
            square = (square * square).astype(jnp.bfloat16)
            diag = lax.dot_general(
                side_ref[EXTRA:, :], square, NN, preferred_element_type=jnp.float32
            )
            other = per_chunk + block
            for trait in range(nx):
                cross_own[trait, turn, :, here] = acc[
                    trait * nlead : (trait + 1) * nlead, :
                ].astype(jnp.bfloat16)
                small_own[trait, turn, block : block + 1, :] = acc[
                    last + trait : last + trait + 1, :
                ]
                small_own[trait, turn, other : other + 1, :] = diag[trait : trait + 1, :]
        for i in range(nx - 1):
            for copy in x_copies(i, turn):
                copy.start()
        return carry

    lax.fori_loop(0, nz, multiply, 0)
    gram = mid_gram[...]
    for d in range(1, nz):
        z_gram_copy(d).wait_recv()
        gram = gram + z_gram[d]
    down = lax.broadcasted_iota(jnp.int32, (nlead, nlead), 0)
    across = lax.broadcasted_iota(jnp.int32, (nlead, nlead), 1)
    eye = down == across
    tall = lax.broadcasted_iota(jnp.int32, (nlead, 2 * nlead), 0)
    wide = lax.broadcasted_iota(jnp.int32, (nlead, 2 * nlead), 1)
    below = lax.broadcasted_iota(jnp.int32, (nlead, 1), 0)
    state = tuple(
        jnp.concatenate(
            [gram[:nlead, r * nlead : (r + 1) * nlead], eye.astype(jnp.float32)], axis=1
        )
        for r in range(nregion)
    )
    lead_score = gram[nlead : nlead + 1, :]

    def eliminate(j, matrix):
        row = jnp.sum(jnp.where(tall == j, matrix, 0.0), axis=0, keepdims=True)
        col = jnp.sum(jnp.where(wide == j, matrix, 0.0), axis=1, keepdims=True)
        pivot = jnp.sum(jnp.where(below == j, col, 0.0), axis=0, keepdims=True)
        return matrix - jnp.where(below > j, col / pivot, 0.0) * row

    def combine(step, state):
        for part in range(nlead // nz):
            state = tuple(eliminate(step * (nlead // nz) + part, matrix) for matrix in state)
        turn = turn_of(step)[0]
        cross = cross_own[x, turn].astype(jnp.float32)
        small = small_own[x, turn]
        for i in range(nx - 1):
            for copy in x_copies(i, turn):
                copy.wait_recv()
            cross = cross + x_cross[i, turn].astype(jnp.float32)
            small = small + x_small[i, turn]
        mid_small[turn] = small

        @pl.when(turn > 0)
        def _():
            mid_cross[turn] = cross.astype(jnp.bfloat16)
            for copy in z_copies(turn):
                copy.start()

        @pl.when(turn == 0)
        def _():
            cross_sum[...] = cross

        return state

    state = lax.fori_loop(0, nz, combine, state)
    for r in range(nregion):
        lower = state[r][:, nlead:]
        pivot = 1.0 / jnp.sum(jnp.where(eye, state[r][:, :nlead], 0.0), axis=1, keepdims=True)
        score = lead_score[:, r * nlead : (r + 1) * nlead]
        inverse[r] = lower
        pivots[r] = jnp.broadcast_to(pivot, (nlead, VB))
        target[r] = jnp.broadcast_to(
            jnp.sum(lower * score, axis=1, keepdims=True) * pivot, (nlead, VB)
        )
    small = mid_small[0]
    cross = cross_sum[...]
    for d in range(1, nz):
        for copy in z_copies(d):
            copy.wait_recv()
        small = small + z_small[d]
        cross = cross + z_cross[d].astype(jnp.float32)
    result[...] = jnp.zeros_like(result)
    for block in range(per_chunk):
        region = region_ref[z * per_chunk + block]
        other = per_chunk + block
        solved = lax.dot_general(
            inverse[region],
            cross[:, block * VB : (block + 1) * VB],
            NN,
            preferred_element_type=jnp.float32,
            precision=lax.Precision.HIGHEST,
        )
        fit = jnp.sum(solved * target[region], axis=0, keepdims=True)
        used = jnp.sum(solved * solved * pivots[region], axis=0, keepdims=True)
        result[block : block + 1, :] = (small[block : block + 1, :] - fit) / math.sqrt(total)
        result[other : other + 1, :] = (small[other : other + 1, :] - used) / total

    first = [
        remote(result, lane.at[z], sent_r.at[i], got_r.at[i], peer)
        for i, peer in enumerate(zpeers)
    ]
    for copy in first:
        copy.start()
    for d in range(1, nz):
        first[d - 1].wait_recv()
        whole[x, lax.rem(z + nz - d, nz)] = lane[lax.rem(z + nz - d, nz)]
    whole[x, z] = result[...]
    second = [
        remote(whole.at[x], whole.at[x], sent_r.at[nz - 1 + i], got_r.at[nz - 1 + i], peer)
        for i, peer in enumerate(xpeers)
    ]
    for copy in second:
        copy.start()
    for copy in second:
        copy.wait_recv()
    for trait in range(nx):
        for chunk in range(nz):
            tile = whole[trait, chunk]
            for block in range(per_chunk):
                at = (chunk * per_chunk + block) * VB
                scores_ref[trait : trait + 1, at : at + VB] = tile[block : block + 1, :]
                variances_ref[trait : trait + 1, at : at + VB] = tile[
                    per_chunk + block : per_chunk + block + 1, :
                ]
    for copy in first + second:
        copy.wait_send()
    for i in range(nx - 1):
        x_gram_copy(i).wait_send()
        for turn in range(nz):
            for copy in x_copies(i, turn):
                copy.wait_send()
    for d in range(1, nz):
        z_gram_copy(d).wait_send()
        for copy in z_copies(d):
            copy.wait_send()


def conditional(regions, slot, incoming, side, genotypes, nx, nregion, nz, total):
    samples, local_vars = genotypes.shape
    nlead = slot.shape[0] // nregion
    chunk = local_vars // nz
    rows = nx * nlead + EXTRA
    vmem = pl.BlockSpec(memory_space=pltpu.VMEM)
    cross = lambda *lead: pltpu.VMEM(lead + (nlead, chunk), jnp.bfloat16)
    small = lambda *lead: pltpu.VMEM(lead + (8, VB), jnp.float32)
    gram = lambda *lead: pltpu.VMEM(lead + (nlead + 8, nregion * nlead), jnp.float32)
    return pl.pallas_call(
        functools.partial(reduce_kernel, total),
        in_specs=[
            pl.BlockSpec(memory_space=pltpu.SMEM),
            vmem,
            vmem,
            vmem,
            pl.BlockSpec(memory_space=pl.ANY),
        ],
        out_specs=[vmem] * 2,
        out_shape=[jax.ShapeDtypeStruct((nx, local_vars), jnp.float32)] * 2,
        scratch_shapes=[
            pltpu.VMEM((nregion * nlead, samples), jnp.bfloat16),
            pltpu.VMEM((nregion, rows, samples), jnp.bfloat16),
            pltpu.VMEM((2, samples, chunk), jnp.bfloat16),
            cross(nx, nz),
            small(nx, nz),
            gram(nx),
            cross(nx - 1, nz),
            small(nx - 1, nz),
            gram(nx - 1),
            cross(nz),
            small(nz),
            gram(),
            cross(nz),
            small(nz),
            gram(nz),
            pltpu.VMEM((nlead, chunk), jnp.float32),
            pltpu.VMEM((nregion, nlead, nlead), jnp.float32),
            pltpu.VMEM((nregion, nlead, VB), jnp.float32),
            pltpu.VMEM((nregion, nlead, VB), jnp.float32),
            small(),
            small(nz),
            small(nx, nz),
            pltpu.SemaphoreType.DMA((2,)),
            pltpu.SemaphoreType.DMA((2, nx - 1, nz + 1)),
            pltpu.SemaphoreType.DMA((2, nx - 1, nz + 1)),
            pltpu.SemaphoreType.DMA((3, nz)),
            pltpu.SemaphoreType.DMA((3, nz)),
            pltpu.SemaphoreType.DMA((nx + nz - 2,)),
            pltpu.SemaphoreType.DMA((nx + nz - 2,)),
        ],
        compiler_params=pltpu.CompilerParams(
            collective_id=0, has_side_effects=True, vmem_limit_bytes=48 * 1024 * 1024
        ),
        name="conditional_scores",
    )(regions, slot, incoming, side, genotypes)


def body(genotypes, residuals, weights, block_regions, leads):
    samples, local_vars = genotypes.shape
    nvar = lax.axis_size("var")
    nsamp = lax.axis_size("samp")
    myself = lax.axis_index("var")
    nregion = leads.shape[0] // nvar
    nlead = leads.shape[1]
    traits = residuals.shape[1]
    nchunk = nsamp // traits
    slots = nregion * nlead
    total = samples * nsamp
    listed = leads.reshape(nvar, slots)
    incoming = gather(listed, genotypes)
    mine = lax.dynamic_index_in_dim(listed, myself, 0, keepdims=False)
    source = mine // local_vars
    order = jnp.arange(slots, dtype=jnp.int32)
    earlier = (source[:, None] == source[None, :]) & (order[None, :] < order[:, None])
    slot = source[:, None] * HOST + jnp.sum(earlier.astype(jnp.int32), axis=1, keepdims=True)
    pad = jnp.zeros((EXTRA - traits, samples), jnp.bfloat16)
    side = jnp.concatenate([residuals.T, pad, weights.T, pad], axis=0)
    scores, variances = conditional(
        block_regions, slot, incoming, side, genotypes, traits, nregion, nchunk, total
    )
    return (scores, variances)


def solution(mesh):
    in_specs = (P("samp", "var"), P("samp", None), P("samp", None), P("var"), P())
    out_specs = (P(None, "var"), P(None, "var"))
    return jax.shard_map(body, mesh=mesh, in_specs=in_specs, out_specs=out_specs, check_vma=False)
```

```python
import functools
import math

import jax
import jax.numpy as jnp
from jax import lax
from jax.experimental import pallas as pl
from jax.experimental.pallas import tpu as pltpu
from jax.sharding import PartitionSpec as P

VB = 128
HOST = 32
NT = (((1,), (1,)), ((), ()))
NN = (((1,), (0,)), ((), ()))
EXTRA = 16
DIRECT, MERGED, RELAY = range(3)


def greet(axis, peers):
    barrier = pltpu.get_barrier_semaphore()
    for peer in peers:
        pl.semaphore_signal(
            barrier, inc=1, device_id={axis: peer}, device_id_type=pl.DeviceIdType.MESH
        )


def hear(peers):
    pl.semaphore_wait(pltpu.get_barrier_semaphore(), len(peers))


def gather_kernel(listed_ref, geno_ref, out_ref, onehot, leaving, landed, sent, got):
    nvar, slots = listed_ref.shape
    local_vars = geno_ref.shape[1]
    tile = geno_ref.shape[0]
    ntile = leaving.shape[0]
    step = pl.program_id(0)
    me = lax.axis_index("var")
    peers = [lax.rem(me + d, nvar) for d in range(1, nvar)]

    @pl.when(step == 0)
    def _():
        greet("var", peers)
        base = me * local_vars
        offset = listed_ref[...] - base
        hosted = (offset >= 0) & (offset < local_vars)
        before = lax.broadcasted_iota(jnp.int32, (slots, slots), 0) < lax.broadcasted_iota(
            jnp.int32, (slots, slots), 1
        )
        rank = lax.dot_general(
            hosted.astype(jnp.float32),
            before.astype(jnp.float32),
            NN,
            preferred_element_type=jnp.float32,
        ).astype(jnp.int32)
        rank = jnp.where(hosted, rank, HOST)
        place = lax.broadcasted_iota(jnp.int32, (HOST, slots), 0)
        lanes = lax.broadcasted_iota(jnp.int32, (HOST, local_vars), 1)
        for owner in range(nvar):
            match = rank[owner : owner + 1, :] == place
            picked = jnp.sum(
                jnp.where(match, offset[owner : owner + 1, :], 0), axis=1, keepdims=True
            )
            onehot[owner * HOST : (owner + 1) * HOST, :] = (
                (lanes == picked).astype(jnp.float32).astype(jnp.bfloat16)
            )
        hear(peers)

    found = lax.dot_general(
        onehot[...], geno_ref[...], NT, preferred_element_type=jnp.float32
    ).astype(jnp.bfloat16)
    for owner in range(nvar):
        leaving[step, owner] = found[owner * HOST : (owner + 1) * HOST, :]

    def copy_to(turn, i):
        return pltpu.make_async_remote_copy(
            src_ref=leaving.at[turn, peers[i]],
            dst_ref=landed.at[turn, i],
            send_sem=sent.at[turn, i],
            recv_sem=got.at[turn, i],
            device_id={"var": peers[i]},
            device_id_type=pl.DeviceIdType.MESH,
        )

    for i in range(nvar - 1):
        copy_to(step, i).start()

    @pl.when(step == ntile - 1)
    def _():
        for turn in range(ntile):
            at = slice(turn * tile, (turn + 1) * tile)
            out_ref[me, :, at] = leaving[turn, me]
            for i in range(nvar - 1):
                copy_to(turn, i).wait_recv()
                out_ref[lax.rem(me + nvar - 1 - i, nvar), :, at] = landed[turn, i]
        for turn in range(ntile):
            for i in range(nvar - 1):
                copy_to(turn, i).wait_send()


def gather(listed, genotypes, tile=256):
    samples, local_vars = genotypes.shape
    nvar, slots = listed.shape
    rows = nvar * HOST
    ntile = samples // tile
    found = pl.pallas_call(
        gather_kernel,
        grid=(ntile,),
        in_specs=[
            pl.BlockSpec((nvar, slots), lambda i: (0, 0)),
            pl.BlockSpec((tile, local_vars), lambda i: (i, 0)),
        ],
        out_specs=pl.BlockSpec((nvar, HOST, samples), lambda i: (0, 0, 0)),
        out_shape=jax.ShapeDtypeStruct((nvar, HOST, samples), jnp.bfloat16),
        scratch_shapes=[
            pltpu.VMEM((rows, local_vars), jnp.bfloat16),
            pltpu.VMEM((ntile, nvar, HOST, tile), jnp.bfloat16),
            pltpu.VMEM((ntile, nvar - 1, HOST, tile), jnp.bfloat16),
            pltpu.SemaphoreType.DMA((ntile, nvar - 1)),
            pltpu.SemaphoreType.DMA((ntile, nvar - 1)),
        ],
        compiler_params=pltpu.CompilerParams(collective_id=2, has_side_effects=True),
        name="lead_exchange",
    )(listed, genotypes)
    return found.reshape(rows, samples)


def places(nx, nz):
    me = lax.axis_index("samp")
    x, z = lax.rem(me, nx), lax.div(me, nx)
    xpeers = [z * nx + lax.rem(x + d, nx) for d in range(1, nx)]
    zpeers = [lax.rem(z + d, nz) * nx + x for d in range(1, nz)]
    return x, z, xpeers, zpeers


def reduce_kernel(
    total,
    region_ref,
    slot_ref,
    incoming_ref,
    side_ref,
    geno_ref,
    scores_ref,
    variances_ref,
    lead,
    weighted,
    cols_buf,
    cross_own,
    small_own,
    gram_own,
    x_cross,
    x_merge,
    x_small,
    x_gram,
    mid_cross,
    mid_small,
    mid_gram,
    z_cross,
    z_small,
    z_gram,
    cross_sum,
    inverse,
    pivots,
    target,
    result,
    lane,
    whole,
    fetched,
    sent_x,
    got_x,
    sent_z,
    got_z,
    sent_r,
    got_r,
):
    nx, nz = cross_own.shape[:2]
    nregion, rows, samples = weighted.shape
    nlead = lead.shape[0] // nregion
    chunk_cols = cols_buf.shape[2]
    per_chunk = chunk_cols // VB
    last = nx * nlead
    x, z, xpeers, zpeers = places(nx, nz)
    greet("samp", xpeers + zpeers)

    def turn_of(step):
        turn = lax.rem(step + nz // 2, nz)
        return turn, lax.rem(z + turn, nz)

    def fetch(step):
        chunk = turn_of(step)[1]
        start = pl.multiple_of(chunk * chunk_cols, VB)
        slot = lax.rem(step, 2)
        return pltpu.make_async_copy(
            geno_ref.at[:, pl.ds(start, chunk_cols)], cols_buf.at[slot], fetched.at[slot]
        )

    def remote(source, target, sent, got, peer):
        return pltpu.make_async_remote_copy(
            src_ref=source,
            dst_ref=target,
            send_sem=sent,
            recv_sem=got,
            device_id={"samp": peer},
            device_id_type=pl.DeviceIdType.MESH,
        )

    def x_small_copy(i, turn):
        return remote(
            small_own.at[lax.rem(x + i + 1, nx), turn],
            x_small.at[i, turn],
            sent_x.at[1, i, turn],
            got_x.at[1, i, turn],
            xpeers[i],
        )

    def x_copy(kind, turn):
        ahead = 1 + (nx - 2) * lax.rem(turn, 2)
        front, back, far = (lax.rem(x + d, nx) for d in (ahead, nx - ahead, 2))
        source, peer = (
            (cross_own.at[back, turn], back),
            (x_merge.at[turn], front),
            (cross_own.at[far, turn], front),
        )[kind]
        return remote(
            source,
            x_cross.at[kind, turn],
            sent_x.at[0, kind, turn],
            got_x.at[0, kind, turn],
            z * nx + peer,
        )

    def pass_on(step):
        turn = turn_of(step)[0]
        front = lax.rem(x + 1 + (nx - 2) * lax.rem(turn, 2), nx)
        x_copy(RELAY, turn).wait_recv()
        x_merge[turn] = (
            cross_own[front, turn].astype(jnp.float32) + x_cross[2, turn].astype(jnp.float32)
        ).astype(jnp.bfloat16)
        x_copy(MERGED, turn).start()

    def x_gram_copy(i):
        trait = lax.rem(x + i + 1, nx)
        return remote(
            gram_own.at[trait], x_gram.at[i], sent_x.at[0, i, nz], got_x.at[0, i, nz], xpeers[i]
        )

    def z_copies(turn):
        peer = lax.rem(z + turn, nz) * nx + x
        return [
            remote(
                mid_cross.at[turn], z_cross.at[turn], sent_z.at[0, turn], got_z.at[0, turn], peer
            ),
            remote(
                mid_small.at[turn], z_small.at[turn], sent_z.at[1, turn], got_z.at[1, turn], peer
            ),
        ]

    def z_gram_copy(d):
        return remote(
            mid_gram, z_gram.at[d], sent_z.at[2, d], got_z.at[2, d], zpeers[d - 1]
        )

    fetch(0).start()
    slots = incoming_ref.shape[0]
    pick = (
        lax.broadcasted_iota(jnp.int32, (nregion * nlead, slots), 1) == slot_ref[...]
    ).astype(jnp.float32).astype(jnp.bfloat16)
    lead[...] = lax.dot_general(
        pick, incoming_ref[...], NN, preferred_element_type=jnp.float32
    ).astype(jnp.bfloat16)
    for region in range(nregion):
        cols = lead[region * nlead : (region + 1) * nlead, :].astype(jnp.float32)
        for trait in range(nx):
            scale = side_ref[EXTRA + trait : EXTRA + trait + 1, :].astype(jnp.float32)
            weighted[region, trait * nlead : (trait + 1) * nlead, :] = (cols * scale).astype(
                jnp.bfloat16
            )
        weighted[region, last:, :] = side_ref[:EXTRA, :]
        gram = lax.dot_general(
            weighted[region],
            lead[region * nlead : (region + 1) * nlead, :],
            NT,
            preferred_element_type=jnp.float32,
        )
        there = slice(region * nlead, (region + 1) * nlead)
        for trait in range(nx):
            gram_own[trait, :nlead, there] = gram[trait * nlead : (trait + 1) * nlead, :]
            gram_own[trait, nlead : nlead + 1, there] = gram[last + trait : last + trait + 1, :]
            gram_own[trait, nlead + 1 :, there] = jnp.zeros((7, nlead), jnp.float32)
    small_own[...] = jnp.zeros_like(small_own)
    hear(xpeers + zpeers)
    for i in range(nx - 1):
        x_gram_copy(i).start()

    def multiply(step, carry):
        turn, chunk = turn_of(step)
        slot = lax.rem(step, 2)
        fetch(step).wait()

        @pl.when(step < nz - 1)
        def _():
            fetch(step + 1).start()

        @pl.when(step == nz // 2)
        def _():
            gram = gram_own[x]
            for i in range(nx - 1):
                x_gram_copy(i).wait_recv()
                gram = gram + x_gram[i]
            mid_gram[...] = gram
            for d in range(1, nz):
                z_gram_copy(d).start()

        for block in range(per_chunk):
            here = slice(block * VB, (block + 1) * VB)
            region = region_ref[chunk * per_chunk + block]
            cols = cols_buf[slot, :, here]
            acc = lax.dot_general(weighted[region], cols, NN, preferred_element_type=jnp.float32)
            square = cols.astype(jnp.float32)
            square = (square * square).astype(jnp.bfloat16)
            diag = lax.dot_general(
                side_ref[EXTRA:, :], square, NN, preferred_element_type=jnp.float32
            )
            other = per_chunk + block
            for trait in range(nx):
                cross_own[trait, turn, :, here] = acc[
                    trait * nlead : (trait + 1) * nlead, :
                ].astype(jnp.bfloat16)
                small_own[trait, turn, block : block + 1, :] = acc[
                    last + trait : last + trait + 1, :
                ]
                small_own[trait, turn, other : other + 1, :] = diag[trait : trait + 1, :]
        x_copy(RELAY, turn).start()
        x_copy(DIRECT, turn).start()
        for i in range(nx - 1):
            x_small_copy(i, turn).start()

        @pl.when(step > 0)
        def _():
            pass_on(step - 1)

        return carry

    lax.fori_loop(0, nz, multiply, 0)
    pass_on(nz - 1)
    gram = mid_gram[...]
    for d in range(1, nz):
        z_gram_copy(d).wait_recv()
        gram = gram + z_gram[d]
    down = lax.broadcasted_iota(jnp.int32, (nlead, nlead), 0)
    across = lax.broadcasted_iota(jnp.int32, (nlead, nlead), 1)
    eye = down == across
    tall = lax.broadcasted_iota(jnp.int32, (nlead, 2 * nlead), 0)
    wide = lax.broadcasted_iota(jnp.int32, (nlead, 2 * nlead), 1)
    below = lax.broadcasted_iota(jnp.int32, (nlead, 1), 0)
    state = tuple(
        jnp.concatenate(
            [gram[:nlead, r * nlead : (r + 1) * nlead], eye.astype(jnp.float32)], axis=1
        )
        for r in range(nregion)
    )
    lead_score = gram[nlead : nlead + 1, :]

    def eliminate(j, matrix):
        row = jnp.sum(jnp.where(tall == j, matrix, 0.0), axis=0, keepdims=True)
        col = jnp.sum(jnp.where(wide == j, matrix, 0.0), axis=1, keepdims=True)
        pivot = jnp.sum(jnp.where(below == j, col, 0.0), axis=0, keepdims=True)
        return matrix - jnp.where(below > j, col / pivot, 0.0) * row

    def combine(step, state):
        for part in range(nlead // nz):
            state = tuple(eliminate(step * (nlead // nz) + part, matrix) for matrix in state)
        turn = turn_of(step)[0]
        cross = cross_own[x, turn].astype(jnp.float32)
        small = small_own[x, turn]
        for kind in (DIRECT, MERGED):
            x_copy(kind, turn).wait_recv()
            cross = cross + x_cross[kind, turn].astype(jnp.float32)
        for i in range(nx - 1):
            x_small_copy(i, turn).wait_recv()
            small = small + x_small[i, turn]
        mid_small[turn] = small

        @pl.when(turn > 0)
        def _():
            mid_cross[turn] = cross.astype(jnp.bfloat16)
            for copy in z_copies(turn):
                copy.start()

        @pl.when(turn == 0)
        def _():
            cross_sum[...] = cross

        return state

    state = lax.fori_loop(0, nz, combine, state)
    for r in range(nregion):
        lower = state[r][:, nlead:]
        pivot = 1.0 / jnp.sum(jnp.where(eye, state[r][:, :nlead], 0.0), axis=1, keepdims=True)
        score = lead_score[:, r * nlead : (r + 1) * nlead]
        inverse[r] = lower
        pivots[r] = jnp.broadcast_to(pivot, (nlead, VB))
        target[r] = jnp.broadcast_to(
            jnp.sum(lower * score, axis=1, keepdims=True) * pivot, (nlead, VB)
        )
    small = mid_small[0]
    cross = cross_sum[...]
    for d in range(1, nz):
        for copy in z_copies(d):
            copy.wait_recv()
        small = small + z_small[d]
        cross = cross + z_cross[d].astype(jnp.float32)
    result[...] = jnp.zeros_like(result)
    for block in range(per_chunk):
        region = region_ref[z * per_chunk + block]
        other = per_chunk + block
        solved = lax.dot_general(
            inverse[region],
            cross[:, block * VB : (block + 1) * VB],
            NN,
            preferred_element_type=jnp.float32,
            precision=lax.Precision.HIGHEST,
        )
        fit = jnp.sum(solved * target[region], axis=0, keepdims=True)
        used = jnp.sum(solved * solved * pivots[region], axis=0, keepdims=True)
        result[block : block + 1, :] = (small[block : block + 1, :] - fit) / math.sqrt(total)
        result[other : other + 1, :] = (small[other : other + 1, :] - used) / total

    first = [
        remote(result, lane.at[z], sent_r.at[i], got_r.at[i], peer)
        for i, peer in enumerate(zpeers)
    ]
    for copy in first:
        copy.start()
    for d in range(1, nz):
        first[d - 1].wait_recv()
        whole[x, lax.rem(z + nz - d, nz)] = lane[lax.rem(z + nz - d, nz)]
    whole[x, z] = result[...]
    second = [
        remote(whole.at[x], whole.at[x], sent_r.at[nz - 1 + i], got_r.at[nz - 1 + i], peer)
        for i, peer in enumerate(xpeers)
    ]
    for copy in second:
        copy.start()
    for copy in second:
        copy.wait_recv()
    for trait in range(nx):
        for chunk in range(nz):
            tile = whole[trait, chunk]
            for block in range(per_chunk):
                at = (chunk * per_chunk + block) * VB
                scores_ref[trait : trait + 1, at : at + VB] = tile[block : block + 1, :]
                variances_ref[trait : trait + 1, at : at + VB] = tile[
                    per_chunk + block : per_chunk + block + 1, :
                ]
    for copy in first + second:
        copy.wait_send()
    for i in range(nx - 1):
        x_gram_copy(i).wait_send()
        for turn in range(nz):
            x_small_copy(i, turn).wait_send()
    for turn in range(nz):
        for kind in (DIRECT, MERGED, RELAY):
            x_copy(kind, turn).wait_send()
    for d in range(1, nz):
        z_gram_copy(d).wait_send()
        for copy in z_copies(d):
            copy.wait_send()


def conditional(regions, slot, incoming, side, genotypes, nx, nregion, nz, total):
    samples, local_vars = genotypes.shape
    nlead = slot.shape[0] // nregion
    chunk = local_vars // nz
    rows = nx * nlead + EXTRA
    vmem = pl.BlockSpec(memory_space=pltpu.VMEM)
    cross = lambda *lead: pltpu.VMEM(lead + (nlead, chunk), jnp.bfloat16)
    small = lambda *lead: pltpu.VMEM(lead + (8, VB), jnp.float32)
    gram = lambda *lead: pltpu.VMEM(lead + (nlead + 8, nregion * nlead), jnp.float32)
    return pl.pallas_call(
        functools.partial(reduce_kernel, total),
        in_specs=[
            pl.BlockSpec(memory_space=pltpu.SMEM),
            vmem,
            vmem,
            vmem,
            pl.BlockSpec(memory_space=pl.ANY),
        ],
        out_specs=[vmem] * 2,
        out_shape=[jax.ShapeDtypeStruct((nx, local_vars), jnp.float32)] * 2,
        scratch_shapes=[
            pltpu.VMEM((nregion * nlead, samples), jnp.bfloat16),
            pltpu.VMEM((nregion, rows, samples), jnp.bfloat16),
            pltpu.VMEM((2, samples, chunk), jnp.bfloat16),
            cross(nx, nz),
            small(nx, nz),
            gram(nx),
            cross(nx - 1, nz),
            cross(nz),
            small(nx - 1, nz),
            gram(nx - 1),
            cross(nz),
            small(nz),
            gram(),
            cross(nz),
            small(nz),
            gram(nz),
            pltpu.VMEM((nlead, chunk), jnp.float32),
            pltpu.VMEM((nregion, nlead, nlead), jnp.float32),
            pltpu.VMEM((nregion, nlead, VB), jnp.float32),
            pltpu.VMEM((nregion, nlead, VB), jnp.float32),
            small(),
            small(nz),
            small(nx, nz),
            pltpu.SemaphoreType.DMA((2,)),
            pltpu.SemaphoreType.DMA((2, nx - 1, nz + 1)),
            pltpu.SemaphoreType.DMA((2, nx - 1, nz + 1)),
            pltpu.SemaphoreType.DMA((3, nz)),
            pltpu.SemaphoreType.DMA((3, nz)),
            pltpu.SemaphoreType.DMA((nx + nz - 2,)),
            pltpu.SemaphoreType.DMA((nx + nz - 2,)),
        ],
        compiler_params=pltpu.CompilerParams(
            collective_id=0, has_side_effects=True, vmem_limit_bytes=48 * 1024 * 1024
        ),
        name="conditional_scores",
    )(regions, slot, incoming, side, genotypes)


def body(genotypes, residuals, weights, block_regions, leads):
    samples, local_vars = genotypes.shape
    nvar = lax.axis_size("var")
    nsamp = lax.axis_size("samp")
    myself = lax.axis_index("var")
    nregion = leads.shape[0] // nvar
    nlead = leads.shape[1]
    traits = residuals.shape[1]
    nchunk = nsamp // traits
    slots = nregion * nlead
    total = samples * nsamp
    listed = leads.reshape(nvar, slots)
    incoming = gather(listed, genotypes)
    mine = lax.dynamic_index_in_dim(listed, myself, 0, keepdims=False)
    source = mine // local_vars
    order = jnp.arange(slots, dtype=jnp.int32)
    earlier = (source[:, None] == source[None, :]) & (order[None, :] < order[:, None])
    slot = source[:, None] * HOST + jnp.sum(earlier.astype(jnp.int32), axis=1, keepdims=True)
    pad = jnp.zeros((EXTRA - traits, samples), jnp.bfloat16)
    side = jnp.concatenate([residuals.T, pad, weights.T, pad], axis=0)
    scores, variances = conditional(
        block_regions, slot, incoming, side, genotypes, traits, nregion, nchunk, total
    )
    return (scores, variances)


def solution(mesh):
    in_specs = (P("samp", "var"), P("samp", None), P("samp", None), P("var"), P())
    out_specs = (P(None, "var"), P(None, "var"))
    return jax.shard_map(body, mesh=mesh, in_specs=in_specs, out_specs=out_specs, check_vma=False)
```
